512 devices in a mesh: lat: 16 (over y_lo, x, core), lon: 32 (over z, y_hi).
Axes of the slice: x: 4, y: 8 (y_hi: 4, y_lo: 2; y = y_hi * 2 + y_lo), z: 8, core: 2. Of those that a mesh axis runs over, the one named last changes fastest.
Arguments:
- features: float32 [4, 96, 384, 192], P(None, 'lat', 'lon'), may hold values from -460 to 460
- cotangent: float32 [4, 96, 384, 192], P(None, 'lat', 'lon'), may hold values from -6 to 6
- norm_gain: float32 [192], replicated, may hold values from 0.1 to 1.9
- norm_shift: float32 [192], replicated, may hold values from -3 to 3
- qkv_weight: float32 [192, 576], replicated, may hold values from -0.4375 to 0.4375
- out_weight: float32 [192, 192], replicated, may hold values from -0.4375 to 0.4375
- bias_table: float32 [16, 2, 6, 23, 144], P('lat'), may hold values from -6 to 305
Outputs:
- grad_features: float32 [4, 96, 384, 192], P(None, 'lat', 'lon')
- grad_weights: float32 [192, 768], P('lat', 'lon')
- grad_bias: float32 [16, 2, 6, 23, 144], P('lat')
- grad_norm: float32 [2, 192], replicated
The draws below stay inside these ranges and needn't reach their ends.
All inputs are finite; a program needn't handle non-finite values.
Results may differ from the reference program's by a relative error of at most 0.0003.
Values sent between devices are 32-bit elements; how exact they have to be, the bound alone decides.
A program may use at most 128 MiB of HBM per device.

```python
import math
import jax
import jax.numpy as jnp
from jax import lax

D = 192
HEADS = 6
HEAD = 32
ZP = 4
WZ = 2
WLAT = 6
WLON = 12
NLAT = 96
NLON = 384
LATW = 16
PW = 2
WIN = 144
LONREL = 23
PAIRS = 144
TOKENS = 147456


def draw_features(key, part):
    first, second, third, fourth = jax.random.split(key, 4)
    shape = (ZP, NLAT, NLON, D)
    base = jnp.clip(jax.random.normal(first, shape, jnp.float32), -4.0, 4.0)
    row_scale = jnp.exp(jax.random.uniform(second, (ZP, NLAT, NLON, 1), jnp.float32, 0.0, math.log(10.0)))
    column_scale = jnp.exp(jax.random.uniform(third, (D,), jnp.float32, 0.0, math.log(10.0)))
    centre = jnp.clip(jax.random.normal(fourth, (D,), jnp.float32), -3.0, 3.0) * 2.0
    return row_scale * (base * column_scale + centre)


def draw_bias_table(key, part):
    first = jax.random.fold_in(key, 0)
    shape = (LATW, PW, HEADS, LONREL, PAIRS)
    base = jnp.clip(jax.random.normal(first, shape, jnp.float32), -6.0, 6.0)
    return base


def steps_of(rng, shape, pieces, smallest, top_value):
    def one(position, blocks):
        draws = jax.random.uniform(jax.random.fold_in(jax.random.fold_in(rng, 6), position), (blocks,), jnp.float32, smallest / len(pieces), top_value / len(pieces))
        return jnp.repeat(jnp.exp(draws), shape[position] // blocks).reshape((-1,) + (1,) * (len(shape) - position - 1))

    level = one(*pieces[0])
    for cut in pieces[1:]:
        level = level * one(*cut)
    return level


def scatter_about(rng, dims, spread, most, cuts=(), held_as=jnp.bfloat16):
    entries = spread * jax.random.normal(rng, dims, jnp.float32)
    if cuts:
        entries = entries * steps_of(rng, dims, cuts, -0.22, 0.18)
    return jnp.clip(entries, -most, most).astype(held_as)


def setup_inputs(seed: int = 0) -> dict:
    keys = jax.random.split(jax.random.key(seed), 8)
    features = draw_features(jax.random.fold_in(keys[7], 71), 0)
    cotangent = scatter_about(keys[1], (ZP, NLAT, NLON, D), 1.0, 6.0, ((1, 16), (2, 32)), jnp.float32)
    norm_gain = jnp.clip(1.0 + 0.18 * jax.random.normal(keys[2], (D,), jnp.float32), 0.1, 1.9)
    norm_shift = scatter_about(keys[3], (D,), 0.5, 3.0, (), jnp.float32)
    qkv_weight = scatter_about(keys[4], (D, 3 * D), D ** -0.5, 0.4375, (), jnp.float32)
    out_weight = scatter_about(keys[5], (D, D), D ** -0.5, 0.4375, (), jnp.float32)
    bias_table = draw_bias_table(jax.random.fold_in(keys[7], 71), 0)
    return dict(features=features, cotangent=cotangent, norm_gain=norm_gain, norm_shift=norm_shift, qkv_weight=qkv_weight, out_weight=out_weight, bias_table=bias_table)


EPSILON = 1e-05
HIGH = lax.Precision.HIGHEST

def offset_table():
    columns = jnp.arange(WLON, dtype=jnp.int32)
    offset = columns[None, :] - columns[:, None] + (WLON - 1)
    return (offset[:, :, None] == jnp.arange(LONREL, dtype=jnp.int32)[None, None, :]).astype(jnp.float32)

def level_valid():
    level = jnp.arange(WIN, dtype=jnp.int32) // (WLAT * WLON)
    same_level = level[:, None] == level[None, :]
    window_index = jnp.arange(PW, dtype=jnp.int32)[:, None, None]
    return (window_index > 0) | same_level[None, :, :]

def expand_bias(table, onehot):
    leading = table.shape[:-3]
    split_table = table.reshape(leading + (HEADS, LONREL, WZ, WZ, WLAT, WLAT))
    full_bias = jnp.einsum('...hrijab,xyr->...hiaxjby', split_table, onehot, precision=HIGH)
    return full_bias.reshape(leading + (HEADS, WIN, WIN))

def band_forward(band, gain, shift, qkv_weight, out_weight, table_band):
    onehot = offset_table()
    average = lax.optimization_barrier(jnp.mean(band, -1, keepdims=True))
    centred = band - average
    standard = centred * lax.rsqrt(lax.optimization_barrier(jnp.mean(centred * centred, -1, keepdims=True)) + EPSILON)
    normed = standard * gain + shift
    shifted = jnp.roll(jnp.roll(normed, 1, 0), WLON // 2, 2)
    col_count = shifted.shape[2] // WLON
    windows = shifted.reshape(PW, WZ, WLAT, col_count, WLON, D).transpose(0, 3, 1, 2, 4, 5).reshape(PW, col_count, WIN, D)
    projected = jnp.einsum('pnwd,de->pnwe', windows, qkv_weight, precision=HIGH)
    query_heads = projected[..., :D].reshape(PW, col_count, WIN, HEADS, HEAD)
    key_heads = projected[..., D:2 * D].reshape(PW, col_count, WIN, HEADS, HEAD)
    value_heads = projected[..., 2 * D:].reshape(PW, col_count, WIN, HEADS, HEAD)
    bias_full = expand_bias(table_band, onehot)
    scores = jnp.einsum('pnahe,pnbhe->pnhab', query_heads, key_heads, precision=HIGH) * HEAD ** (-0.5) + bias_full[:, None]
    scores = jnp.where(level_valid()[:, None, None], scores, -jnp.inf)
    attention = jax.nn.softmax(scores, axis=-1)
    mixture = jnp.einsum('pnhab,pnbhe->pnahe', attention, value_heads, precision=HIGH).reshape(PW, col_count, WIN, D)
    output = jnp.einsum('pnwd,de->pnwe', mixture, out_weight, precision=HIGH)
    back = output.reshape(PW, col_count, WZ, WLAT, WLON, D).transpose(0, 2, 3, 1, 4, 5).reshape(ZP, WLAT, col_count * WLON, D)
    return jnp.roll(jnp.roll(back, -(WLON // 2), 2), -1, 0)

def reference(features, cotangent, norm_gain, norm_shift, qkv_weight, out_weight, bias_table):

    def step(carry, index):
        start = (index * WLAT).astype(jnp.int32)
        band = lax.dynamic_slice_in_dim(features, start, WLAT, 1)
        band_grad = lax.dynamic_slice_in_dim(cotangent, start, WLAT, 1)
        table_band = lax.dynamic_index_in_dim(bias_table, index, 0, keepdims=False)
        _, pullback = jax.vjp(band_forward, band, norm_gain, norm_shift, qkv_weight, out_weight, table_band)
        grad_band, grad_gain, grad_shift, grad_qkv, grad_out, grad_table = pullback(band_grad)
        carry = (carry[0] + grad_gain, carry[1] + grad_shift, carry[2] + grad_qkv, carry[3] + grad_out)
        return (carry, (grad_band + band_grad, grad_table))
    start_carry = (jnp.zeros((D,), jnp.float32), jnp.zeros((D,), jnp.float32), jnp.zeros((D, 3 * D), jnp.float32), jnp.zeros((D, D), jnp.float32))
    carry, (grad_bands, grad_bias) = lax.scan(step, start_carry, jnp.arange(LATW, dtype=jnp.int32))
    grad_features = grad_bands.transpose(1, 0, 2, 3, 4).reshape(ZP, NLAT, NLON, D)
    factor = 1.0 / math.sqrt(TOKENS)
    grad_weights = jnp.concatenate([carry[2], carry[3]], axis=1) * factor
    grad_norm = jnp.stack([carry[0], carry[1]]) * factor
    return (grad_features, grad_weights, grad_bias, grad_norm)
```

```python
import functools

import jax
import jax.numpy as jnp
import numpy as np
from jax import lax
from jax.experimental import pallas as pl
from jax.experimental.pallas import tpu as pltpu
from jax.sharding import PartitionSpec as P

D = 192
HEADS = 6
HEAD = 32
WLAT = 6
WLON = 12
HALF = WLON // 2
PW = 2
LONREL = 23
PAIRS = 144
EPSILON = 1e-05

GROUP = 16
ROWS = WLON * GROUP
HROWS = HALF * GROUP
STACK = HEADS * ROWS
BLOCK = HEADS * GROUP
STRIP = 24 * GROUP
POS = 12
TABW = 896
NEG = -1e30
F32 = jnp.float32
HIGH = lax.Precision.HIGH
MESH = pl.DeviceIdType.MESH
LAT = 16
NZ = 8
NY = 4
VLIM = 60 * 1024 * 1024


def permutation():
    out = np.zeros((POS * 128, TABW), np.float32)
    for n in range(POS):
        j, b = divmod(n, WLAT)
        for h in range(HEADS):
            for i in range(2):
                for a in range(WLAT):
                    p = ((i * 2 + j) * WLAT + a) * WLAT + b
                    col = h * 128 + p if p < 128 else 768 + h * 16 + p - 128
                    out[n * 128 + h * GROUP + i * 8 + a, col] = 1.0
    return out


def mask_strips():
    lane = np.arange(STRIP) % GROUP
    row = np.arange(BLOCK) % GROUP
    j, b, i = lane // 8, lane % 8, row // 8
    padded = np.broadcast_to((b >= WLAT)[None, :], (BLOCK, STRIP))
    other = i[:, None] != j[None, :]
    return np.where(np.stack([padded | other, padded]), NEG, 0.0).astype(np.float32)


def nn(a, b, precision=HIGH):
    return lax.dot_general(a, b, (((1,), (0,)), ((), ())), precision=precision, preferred_element_type=F32)


def nt(a, b, precision=HIGH):
    return lax.dot_general(a, b, (((1,), (1,)), ((), ())), precision=precision, preferred_element_type=F32)


def tn(a, b, precision=HIGH):
    return lax.dot_general(a, b, (((0,), (0,)), ((), ())), precision=precision, preferred_element_type=F32)


def split(x, terms):
    parts = []
    for _ in range(terms):
        part = x.astype(jnp.bfloat16)
        parts.append(part)
        x = x - part.astype(F32)
    return parts


def pack_piece(feat_ref, cot_ref, slabs, first, store):
    for x in range(HALF):
        for i, z in enumerate(slabs):
            f = feat_ref[pl.ds(z * WLAT, WLAT), first + x, :]
            c = cot_ref[pl.ds(z * WLAT, WLAT), first + x, :]
            value = jnp.concatenate(
                [f[:, :128], c[:, :128], f[:, 128:], c[:, 128:]], axis=1
            )
            value = jnp.concatenate([value, jnp.zeros((2, 2 * D), F32)], axis=0)
            store(x * GROUP + i * 8, value)


def halo_kernel(feat_ref, cot_ref, win_ref, to_right, to_left, send_sem, recv_sem):
    lon = lax.axis_index("lon")
    count = NZ * NY
    right, left = lax.rem(lon + 1, count), lax.rem(lon + count - 1, count)
    barrier = pltpu.get_barrier_semaphore()
    for neighbour in (left, right):
        pl.semaphore_signal(barrier, inc=1, device_id={"lon": neighbour}, device_id_type=MESH)

    def into(ref):
        def store(row, value):
            ref[pl.ds(row, 8), :] = value

        return store

    pack_piece(feat_ref, cot_ref, (3, 0), HALF, into(to_right))
    pack_piece(feat_ref, cot_ref, (1, 2), 0, into(to_left))
    pl.semaphore_wait(barrier, 2)
    copies = [
        pltpu.make_async_remote_copy(
            src_ref=to_right,
            dst_ref=win_ref.at[0, pl.ds(0, HROWS)],
            send_sem=send_sem.at[0],
            recv_sem=recv_sem.at[0],
            device_id={"lon": right},
            device_id_type=MESH,
        ),
        pltpu.make_async_remote_copy(
            src_ref=to_left,
            dst_ref=win_ref.at[1, pl.ds(HROWS, HROWS)],
            send_sem=send_sem.at[1],
            recv_sem=recv_sem.at[1],
            device_id={"lon": left},
            device_id_type=MESH,
        ),
    ]
    for copy in copies:
        copy.start()

    def own(c, base):
        def store(row, value):
            win_ref[c, pl.ds(base + row, 8), :] = value

        return store

    pack_piece(feat_ref, cot_ref, (3, 0), 0, own(0, HROWS))
    pack_piece(feat_ref, cot_ref, (1, 2), HALF, own(1, 0))
    for copy in copies:
        copy.wait()


def halo(features, cotangent):
    vmem = pl.BlockSpec(memory_space=pltpu.VMEM)
    return pl.pallas_call(
        halo_kernel,
        out_shape=jax.ShapeDtypeStruct((PW, ROWS, 2 * D), F32),
        in_specs=[vmem] * 2,
        out_specs=vmem,
        scratch_shapes=[
            pltpu.VMEM((HROWS, 2 * D), F32),
            pltpu.VMEM((HROWS, 2 * D), F32),
            pltpu.SemaphoreType.DMA((2,)),
            pltpu.SemaphoreType.DMA((2,)),
        ],
        compiler_params=pltpu.CompilerParams(collective_id=0, has_side_effects=True, vmem_limit_bytes=VLIM),
        name="halo",
    )(features.reshape(4 * WLAT, WLON, D), cotangent.reshape(4 * WLAT, WLON, D))


def head_lane(h, rows):
    lane = lax.broadcasted_iota(jnp.int32, (rows, D), 1)
    return (lane >= h * HEAD) & (lane < (h + 1) * HEAD)


def compute_kernel(
    win_ref, gain_ref, shift_ref, qkv_ref, out_ref, table_ref, perm_ref, mask_ref,
    grad_ref, wsend_ref, bsend_ref,
    strip, turned, qs, gs, scores, dattn, dstrip, lanes,
):
    zero_row = jnp.zeros((1, 128), F32)
    rem_row = jnp.zeros((1, 16), F32)
    mains, rems = [], []
    for c in range(PW):
        main, rem = [], []
        for h in range(HEADS):
            t = table_ref[c, h]
            main.append(jnp.concatenate([t[:, :128], zero_row], axis=0))
            rem.append(jnp.concatenate([t[:, 128:], rem_row], axis=0))
        rem.append(jnp.zeros((24, 32), F32))
        mains.append(jnp.concatenate(main, axis=1))
        rems.append(jnp.concatenate(rem, axis=1))
    table = jnp.concatenate(
        [jnp.concatenate(mains, axis=0), jnp.concatenate(rems, axis=0)], axis=1
    )
    perm = perm_ref[...]
    spread = sum(nt(part, perm, None) for part in split(table, 3))
    for c in range(PW):
        for n in range(POS):
            row = (n // WLAT) * 8 + n % WLAT
            turned[pl.ds(row, 24, stride=GROUP), :] = spread[c * 24 : c * 24 + 24, n * 128 : n * 128 + 128]
        for n in (6, 7, 14, 15):
            turned[pl.ds(n, 24, stride=GROUP), :] = jnp.zeros((24, 128), F32)
        strip[c] = turned[...].T[:BLOCK, :] + mask_ref[c]

    packed = win_ref[...].reshape(PW * ROWS, 2 * D)
    feat = jnp.concatenate([packed[:, :128], packed[:, 256:320]], axis=1)
    cot = jnp.concatenate([packed[:, 128:256], packed[:, 320:384]], axis=1)
    average = jnp.sum(feat, axis=1, keepdims=True) * (1.0 / D)
    centred = feat - average
    inverse = lax.rsqrt(jnp.sum(centred * centred, axis=1, keepdims=True) * (1.0 / D) + EPSILON)
    unit = centred * inverse
    gain = gain_ref[...]
    hidden = unit * gain + shift_ref[...]
    wq, wk, wv = (qkv_ref[:, e * D : (e + 1) * D] for e in range(3))
    wo = out_ref[...]
    scale = HEAD ** (-0.5)
    query = nn(hidden, wq) * scale
    key = nn(hidden, wk)
    value = nn(hidden, wv)
    grad_mix = nt(cot, wo)

    mixtures, grad_q, grad_k, grad_v = [], [], [], []
    for w in range(PW):
        base = w * ROWS
        q_w, k_w, v_w, g_w = (t[base : base + ROWS] for t in (query, key, value, grad_mix))
        for h in range(HEADS):
            keep = head_lane(h, GROUP)
            for x in range(WLON):
                at = pl.ds(x * BLOCK + h * GROUP, GROUP)
                qs[at, :] = jnp.where(keep, q_w[x * GROUP : (x + 1) * GROUP], 0.0)
                gs[at, :] = jnp.where(keep, g_w[x * GROUP : (x + 1) * GROUP], 0.0)
        scores[...] = nt(qs[...], k_w)
        dattn[...] = nt(gs[...], v_w)
        band = strip[w]
        dband = jnp.zeros((BLOCK, STRIP), F32)
        for x in range(WLON):
            at = pl.ds(x * BLOCK, BLOCK)
            move = (WLON - 1 - x) * GROUP
            bias = band if move == 0 else pltpu.roll(band, STRIP - move, 1)
            s = scores[at, :] + bias[:, :ROWS]
            e = jnp.exp(s - jnp.max(s, axis=1, keepdims=True))
            a = e * (1.0 / jnp.sum(e, axis=1, keepdims=True))
            da = dattn[at, :]
            ds = a * (da - jnp.sum(a * da, axis=1, keepdims=True))
            scores[at, :] = a
            dattn[at, :] = ds
            wide = jnp.concatenate([ds, jnp.zeros((BLOCK, STRIP - ROWS), F32)], axis=1)
            dband = dband + (wide if move == 0 else pltpu.roll(wide, move, 1))
        dstrip[w] = dband
        att = scores[...]
        ds = dattn[...]
        grad_k.append(tn(ds, qs[...]))
        grad_v.append(tn(att, gs[...]))
        for source, other, sink in ((att, v_w, mixtures), (ds, k_w, grad_q)):
            qs[...] = nn(source, other)
            pieces = []
            for x in range(WLON):
                total = jnp.zeros((GROUP, D), F32)
                for h in range(HEADS):
                    total = jnp.where(
                        head_lane(h, GROUP), qs[pl.ds(x * BLOCK + h * GROUP, GROUP), :], total
                    )
                pieces.append(total)
            sink.append(jnp.concatenate(pieces, axis=0))

    mixture = jnp.concatenate(mixtures, axis=0)
    dq = jnp.concatenate(grad_q, axis=0) * scale
    dk = jnp.concatenate(grad_k, axis=0)
    dv = jnp.concatenate(grad_v, axis=0)

    gq, gk, gv = tn(hidden, dq), tn(hidden, dk), tn(hidden, dv)
    go = tn(mixture, cot)
    columns = [
        gq[:, :128], gk[:, :128], gv[:, :128], go[:, :128],
        jnp.concatenate([gq[:, 128:], gk[:, 128:]], axis=1),
        jnp.concatenate([gv[:, 128:], go[:, 128:]], axis=1),
    ]
    for l in range(LAT):
        for g in range(6):
            wsend_ref[l, pl.ds(g * 12, 12), :] = columns[g][l * 12 : (l + 1) * 12]

    gh = nt(dq, wq) + nt(dk, wk) + nt(dv, wv)
    ggain = jnp.sum(gh * unit, axis=0, keepdims=True)
    gshift = jnp.sum(gh, axis=0, keepdims=True)
    norm = jnp.concatenate(
        [
            ggain[:, :128], gshift[:, :128],
            jnp.concatenate([ggain[:, 128:], gshift[:, 128:]], axis=1),
            jnp.zeros((5, 128), F32),
        ],
        axis=0,
    )
    for l in range(LAT):
        wsend_ref[l, pl.ds(72, 8), :] = norm
    gu = gh * gain
    mean_gu = jnp.sum(gu, axis=1, keepdims=True) * (1.0 / D)
    mean_uu = jnp.sum(gu * unit, axis=1, keepdims=True) * (1.0 / D)
    grad_ref[...] = (cot + inverse * (gu - mean_gu - unit * mean_uu)).reshape(PW, ROWS, D)

    for c in range(PW):
        turned[:, :BLOCK] = dstrip[c].T
        for n in range(POS):
            row = (n // WLAT) * 8 + n % WLAT
            lanes[pl.ds(c * 24, 24), n * 128 : n * 128 + 128] = turned[pl.ds(row, 24, stride=GROUP), :]
    sums = sum(nn(part, perm, None) for part in split(lanes[...], 2))
    for t in range(7):
        bsend_ref[t] = sums[:, t * 128 : (t + 1) * 128]
    bsend_ref[7] = jnp.zeros((48, 128), F32)


def compute(win, gain, shift, qkv, out, table, perm, mask):
    vmem = pl.BlockSpec(memory_space=pltpu.VMEM)
    return pl.pallas_call(
        compute_kernel,
        out_shape=(
            jax.ShapeDtypeStruct((PW, ROWS, D), F32),
            jax.ShapeDtypeStruct((LAT, 80, 128), F32),
            jax.ShapeDtypeStruct((NZ, 48, 128), F32),
        ),
        in_specs=[vmem] * 8,
        out_specs=(vmem,) * 3,
        scratch_shapes=[
            pltpu.VMEM((PW, BLOCK, STRIP), F32),
            pltpu.VMEM((STRIP, 128), F32),
            pltpu.VMEM((STACK, D), F32),
            pltpu.VMEM((STACK, D), F32),
            pltpu.VMEM((STACK, ROWS), F32),
            pltpu.VMEM((STACK, ROWS), F32),
            pltpu.VMEM((PW, BLOCK, STRIP), F32),
            pltpu.VMEM((48, POS * 128), F32),
        ],
        compiler_params=pltpu.CompilerParams(vmem_limit_bytes=VLIM),
        name="window_math",
    )(win, gain, shift, qkv, out, table, perm, mask)


def reduce_kernel(
    grad_ref, wsend_ref, bsend_ref,
    feat_ref, weight_ref, bias_ref, norm_ref,
    piece, wrecv, brecv, ypart, yrecv, gathered, zsend, zrecv, ysend, last,
    send_w, recv_w, send_b, recv_b, send_y, recv_y, send_g, recv_g,
    send_z, recv_z, send_l, recv_l, send_p, recv_p,
):
    lat, lon = lax.axis_index("lat"), lax.axis_index("lon")
    count = NZ * NY
    z, y = lon // NY, lax.rem(lon, NY)
    right, left = lax.rem(lon + 1, count), lax.rem(lon + count - 1, count)

    def at_lat(i):
        return {"lat": lax.rem(lat + i, LAT)}

    def at_z(i):
        return {"lon": lax.rem(z + i, NZ) * NY + y}

    def at_y(i):
        return {"lon": z * NY + lax.rem(y + i, NY)}

    barrier = pltpu.get_barrier_semaphore()

    def greet(where):
        def body(i, carry):
            pl.semaphore_signal(barrier, inc=1, device_id=where(i), device_id_type=MESH)
            return carry

        return body

    lax.fori_loop(1, LAT, greet(at_lat), 0)
    lax.fori_loop(1, NZ, greet(at_z), 0)
    lax.fori_loop(1, NY, greet(at_y), 0)
    for neighbour in (left, right):
        pl.semaphore_signal(barrier, inc=1, device_id={"lon": neighbour}, device_id_type=MESH)
    pl.semaphore_wait(barrier, LAT - 1 + NZ - 1 + NY - 1 + 2)

    def remote(src, dst, send, recv, device):
        return pltpu.make_async_remote_copy(
            src_ref=src, dst_ref=dst, send_sem=send, recv_sem=recv, device_id=device, device_id_type=MESH
        )

    def exchange(n, mine, where, src, dst, send, recv):
        def start(i, carry):
            other = lax.rem(mine + i, n)
            remote(src(other), dst.at[mine], send.at[i], recv.at[mine], where(i)).start()
            return carry

        lax.fori_loop(1, n, start, 0)

    def finish(n, mine, where, src, dst, send, recv):
        def done(i, carry):
            other = lax.rem(mine + i, n)
            copy = remote(src(other), dst.at[other], send.at[i], recv.at[other], where(i))
            copy.wait_send()
            copy.wait_recv()
            return carry

        lax.fori_loop(1, n, done, 0)

    def total(ref, n):
        return functools.reduce(lambda a, b: a + b, [ref[s] for s in range(n)])

    step_b = (NZ, z, at_z, lambda o: bsend_ref.at[o], brecv, send_b, recv_b)
    step_w = (LAT, lat, at_lat, lambda o: wsend_ref.at[o], wrecv, send_w, recv_w)
    step_y = (NY, y, at_y, lambda o: ypart, yrecv, send_y, recv_y)
    step_g = (NZ, z, at_z, lambda o: gathered.at[z], gathered, send_g, recv_g)
    step_z = (NZ, z, at_z, lambda o: zsend.at[o], zrecv, send_z, recv_z)
    step_l = (NY, y, at_y, lambda o: ysend, last, send_l, recv_l)

    exchange(*step_b)
    exchange(*step_w)
    backs = [
        remote(grad_ref.at[0, pl.ds(0, HROWS)], piece.at[0], send_p.at[0], recv_p.at[0], {"lon": left}),
        remote(grad_ref.at[1, pl.ds(HROWS, HROWS)], piece.at[1], send_p.at[1], recv_p.at[1], {"lon": right}),
    ]
    for copy in backs:
        copy.start()
    brecv[z] = bsend_ref[z]
    wrecv[lat] = wsend_ref[lat]

    finish(*step_b)
    ypart[...] = total(brecv, NZ)
    yrecv[y] = ypart[...]
    exchange(*step_y)

    finish(*step_w)
    block = total(wrecv, LAT)
    norm = block[72:75]
    lane = lax.broadcasted_iota(jnp.int32, (12, 128), 1)
    for t in range(NZ):
        main = block[(t // 2) * 12 : (t // 2) * 12 + 12]
        if t % 2:
            extra = block[48 + (t // 4) * 12 : 60 + (t // 4) * 12]
            tail = pltpu.roll(extra, 32 if (t // 2) % 2 == 0 else 96, 1)
            main = jnp.where(lane < 32, pltpu.roll(main, 32, 1), tail)
        zsend[t, 0:12, :] = main
        zsend[t, 12:15, :] = norm
        zsend[t, 15:16, :] = jnp.zeros((1, 128), F32)
    zrecv[z] = zsend[z]
    exchange(*step_z)

    finish(*step_y)
    gathered[z] = total(yrecv, NY)
    exchange(*step_g)

    finish(*step_z)
    ysend[...] = total(zrecv, NZ)
    last[y] = ysend[...]
    exchange(*step_l)

    for copy in backs:
        copy.wait()
    for x in range(HALF):
        for c, slabs in ((0, (3, 0)), (1, (1, 2))):
            for i, slab in enumerate(slabs):
                row = x * GROUP + i * 8
                own = grad_ref[c, pl.ds((HROWS if c == 0 else 0) + row, 8), :]
                far = piece[c, pl.ds(row, 8), :]
                west, east = (own, far) if c == 0 else (far, own)
                feat_ref[pl.ds(slab * WLAT, WLAT), x, :] = west[:WLAT]
                feat_ref[pl.ds(slab * WLAT, WLAT), HALF + x, :] = east[:WLAT]

    factor = 1.0 / 384.0
    finish(*step_g)
    for h in range(HEADS):
        main = gathered[h]
        rem = gathered[6]
        rem = rem if h == 0 else pltpu.roll(rem, 128 - 16 * h, 1)
        for c in range(PW):
            bias_ref[c, h, :, 0:128] = main[c * 24 : c * 24 + LONREL]
            bias_ref[c, h, :, 128:144] = rem[c * 24 : c * 24 + LONREL, :16]

    finish(*step_l)
    both = total(last, NY) * factor
    rows = both[0:12]
    mine = rows[:, 0:24]
    for t in range(1, NY):
        mine = jnp.where(y == t, pltpu.roll(rows, 128 - 24 * t, 1)[:, 0:24], mine)
    weight_ref[...] = mine
    norm_ref[0:1, 0:128] = both[12:13]
    norm_ref[1:2, 0:128] = both[13:14]
    norm_ref[0:1, 128:192] = both[14:15, 0:64]
    norm_ref[1:2, 128:192] = both[14:15, 64:128]


def reduce(grad, wsend, bsend):
    vmem = pl.BlockSpec(memory_space=pltpu.VMEM)
    dma = pltpu.SemaphoreType.DMA
    sems = []
    for n in (LAT, NZ, NY, NZ, NZ, NY, 2):
        sems += [dma((n,)), dma((n,))]
    return pl.pallas_call(
        reduce_kernel,
        out_shape=(
            jax.ShapeDtypeStruct((4 * WLAT, WLON, D), F32),
            jax.ShapeDtypeStruct((12, 24), F32),
            jax.ShapeDtypeStruct((PW, HEADS, LONREL, PAIRS), F32),
            jax.ShapeDtypeStruct((2, D), F32),
        ),
        in_specs=[vmem] * 3,
        out_specs=(vmem,) * 4,
        scratch_shapes=[
            pltpu.VMEM((2, HROWS, D), F32),
            pltpu.VMEM((LAT, 80, 128), F32),
            pltpu.VMEM((NZ, 48, 128), F32),
            pltpu.VMEM((48, 128), F32),
            pltpu.VMEM((NY, 48, 128), F32),
            pltpu.VMEM((NZ, 48, 128), F32),
            pltpu.VMEM((NZ, 16, 128), F32),
            pltpu.VMEM((NZ, 16, 128), F32),
            pltpu.VMEM((16, 128), F32),
            pltpu.VMEM((NY, 16, 128), F32),
        ] + sems,
        compiler_params=pltpu.CompilerParams(collective_id=1, has_side_effects=True, vmem_limit_bytes=VLIM),
        name="reductions",
    )(grad, wsend, bsend)


def shards(features, cotangent, norm_gain, norm_shift, qkv_weight, out_weight, bias_table):
    win = halo(features, cotangent)
    grad, wsend, bsend = compute(
        win,
        norm_gain.reshape(1, D),
        norm_shift.reshape(1, D),
        qkv_weight,
        out_weight,
        bias_table.reshape(PW, HEADS, LONREL, PAIRS),
        jnp.asarray(permutation(), jnp.bfloat16),
        jnp.asarray(mask_strips()),
    )
    grad_features, grad_weights, grad_bias, grad_norm = reduce(grad, wsend, bsend)
    return (
        grad_features.reshape(features.shape),
        grad_weights,
        grad_bias.reshape(bias_table.shape),
        grad_norm,
    )


def solution(mesh):
    placed = (
        P(None, "lat", "lon", None),
        P(None, "lat", "lon", None),
        P(),
        P(),
        P(),
        P(),
        P("lat", None, None, None, None),
    )
    return jax.shard_map(
        shards,
        mesh=mesh,
        in_specs=placed,
        out_specs=(
            P(None, "lat", "lon", None),
            P("lat", "lon"),
            P("lat", None, None, None, None),
            P(),
        ),
        check_vma=False,
    )
```

```python
import functools

import jax
import jax.numpy as jnp
import numpy as np
from jax import lax
from jax.experimental import pallas as pl
from jax.experimental.pallas import tpu as pltpu
from jax.sharding import PartitionSpec as P

D = 192
HEADS = 6
HEAD = 32
WLAT = 6
WLON = 12
HALF = WLON // 2
PW = 2
LONREL = 23
PAIRS = 144
EPSILON = 1e-05

GROUP = 16
ROWS = WLON * GROUP
HROWS = HALF * GROUP
STACK = HEADS * ROWS
BLOCK = HEADS * GROUP
STRIP = 24 * GROUP
POS = 12
TABW = 896
NEG = -1e30
F32 = jnp.float32
HIGH = lax.Precision.HIGH
MESH = pl.DeviceIdType.MESH
LAT = 16
NK = 8
NZ = 8
NY = 4
VLIM = 32 * 1024 * 1024


def permutation():
    out = np.zeros((POS * 128, TABW), np.float32)
    for n in range(POS):
        j, b = divmod(n, WLAT)
        for h in range(HEADS):
            for i in range(2):
                for a in range(WLAT):
                    p = ((i * 2 + j) * WLAT + a) * WLAT + b
                    col = h * 128 + p if p < 128 else 768 + h * 16 + p - 128
                    out[n * 128 + h * GROUP + i * 8 + a, col] = 1.0
    return out


def mask_strips():
    lane = np.arange(STRIP) % GROUP
    row = np.arange(BLOCK) % GROUP
    j, b, i = lane // 8, lane % 8, row // 8
    padded = np.broadcast_to((b >= WLAT)[None, :], (BLOCK, STRIP))
    other = i[:, None] != j[None, :]
    return np.where(np.stack([padded | other, padded]), NEG, 0.0).astype(np.float32)


def nn(a, b, precision=HIGH):
    return lax.dot_general(a, b, (((1,), (0,)), ((), ())), precision=precision, preferred_element_type=F32)


def nt(a, b, precision=HIGH):
    return lax.dot_general(a, b, (((1,), (1,)), ((), ())), precision=precision, preferred_element_type=F32)


def tn(a, b, precision=HIGH):
    return lax.dot_general(a, b, (((0,), (0,)), ((), ())), precision=precision, preferred_element_type=F32)


def split(x, terms):
    parts = []
    for _ in range(terms):
        part = x.astype(jnp.bfloat16)
        parts.append(part)
        x = x - part.astype(F32)
    return parts


def pack_piece(feat_ref, cot_ref, slabs, first, store):
    for x in range(HALF):
        for i, z in enumerate(slabs):
            f = feat_ref[:, first + x, z, :]
            c = cot_ref[:, first + x, z, :]
            value = jnp.concatenate(
                [f[:, :128], c[:, :128], f[:, 128:], c[:, 128:]], axis=1
            )
            value = jnp.concatenate([value, jnp.zeros((2, 2 * D), F32)], axis=0)
            store(x * GROUP + i * 8, value)


def head_lane(h, rows):
    lane = lax.broadcasted_iota(jnp.int32, (rows, D), 1)
    return (lane >= h * HEAD) & (lane < (h + 1) * HEAD)


def bias_strips(table_ref, perm_ref, mask_ref, turned, strip):
    zero_row = jnp.zeros((1, 128), F32)
    rem_row = jnp.zeros((1, 16), F32)
    mains, rems = [], []
    for c in range(PW):
        main, rem = [], []
        for h in range(HEADS):
            t = table_ref[h, :, c, :]
            main.append(jnp.concatenate([t[:, :128], zero_row], axis=0))
            rem.append(jnp.concatenate([t[:, 128:], rem_row], axis=0))
        rem.append(jnp.zeros((24, 32), F32))
        mains.append(jnp.concatenate(main, axis=1))
        rems.append(jnp.concatenate(rem, axis=1))
    table = jnp.concatenate(
        [jnp.concatenate(mains, axis=0), jnp.concatenate(rems, axis=0)], axis=1
    )
    perm = perm_ref[...]
    spread = sum(nt(part, perm, None) for part in split(table, 3))
    for c in range(PW):
        for n in range(POS):
            row = (n // WLAT) * 8 + n % WLAT
            turned[pl.ds(row, 24, stride=GROUP), :] = spread[c * 24 : c * 24 + 24, n * 128 : n * 128 + 128]
        for n in (6, 7, 14, 15):
            turned[pl.ds(n, 24, stride=GROUP), :] = jnp.zeros((24, 128), F32)
        strip[c] = turned[...].T[:BLOCK, :] + mask_ref[c]


def main_kernel(
    comm,
    feat_ref, cot_ref, gain_ref, shift_ref, qkv_ref, out_ref, table_ref, perm_ref, mask_ref,
    grad_ref, piece, gathered, last,
    win, to_right, to_left, hid, unit, cot, inv, que, key, val, gmx,
    strip, turned, qs, gs, scores, dattn, dstrip, lanes,
    wsend, nsend, bsend, crecv, nrecv, csum, hrecv, brecv, ypart, yrecv, zsend, zrecv, ysend,
    send_p, recv_p, send_c, recv_c, send_h, recv_h, send_b, recv_b, send_y, recv_y, send_g, recv_g,
    send_z, recv_z, send_l, recv_l,
):
    if comm:
        lat, lon = lax.axis_index("lat"), lax.axis_index("lon")
    else:
        lat, lon = jnp.int32(0), jnp.int32(0)
    count = NZ * NY
    z, y = lon // NY, lax.rem(lon, NY)
    k, core = lat // 2, lax.rem(lat, 2)
    right, left = {"lon": lax.rem(lon + 1, count)}, {"lon": lax.rem(lon + count - 1, count)}
    partner = {"lat": k * 2 + 1 - core}

    def at_k(i):
        return {"lat": lax.rem(k + i, NK) * 2 + core}

    def at_z(i):
        return {"lon": lax.rem(z + i, NZ) * NY + y}

    def at_y(i):
        return {"lon": z * NY + lax.rem(y + i, NY)}

    def remote(src, dst, send, recv, device):
        return pltpu.make_async_remote_copy(
            src_ref=src, dst_ref=dst, send_sem=send, recv_sem=recv, device_id=device, device_id_type=MESH
        )

    def start_all(copies):
        for copy in copies if comm else ():
            copy.start()

    def wait_all(copies):
        for copy in copies if comm else ():
            copy.wait()

    def exchange(n, mine, where, src, dst, send, recv):
        def start(i, carry):
            other = lax.rem(mine + i, n)
            remote(src(other), dst.at[mine], send.at[i], recv.at[mine], where(i)).start()
            return carry

        if comm:
            lax.fori_loop(1, n, start, 0)

    def finish(n, mine, where, src, dst, send, recv):
        def done(i, carry):
            other = lax.rem(mine + i, n)
            copy = remote(src(other), dst.at[other], send.at[i], recv.at[other], where(i))
            copy.wait_send()
            copy.wait_recv()
            return carry

        if comm:
            lax.fori_loop(1, n, done, 0)

    def total(ref, n):
        return functools.reduce(lambda a, b: a + b, [ref[s] for s in range(n)])

    if comm:
        barrier = pltpu.get_barrier_semaphore()

        def greet(where):
            def step(i, carry):
                pl.semaphore_signal(barrier, inc=1, device_id=where(i), device_id_type=MESH)
                return carry

            return step

        for device in (left, right, partner):
            pl.semaphore_signal(barrier, inc=1, device_id=device, device_id_type=MESH)
        lax.fori_loop(1, NY, greet(at_y), 0)
        lax.fori_loop(1, NZ, greet(at_z), 0)
        lax.fori_loop(1, NK, greet(at_k), 0)

    def into(ref, base):
        def store(row, value):
            ref[pl.ds(base + row, 8), :] = value

        return store

    pack_piece(feat_ref, cot_ref, (3, 0), HALF, into(to_right, 0))
    pack_piece(feat_ref, cot_ref, (1, 2), 0, into(to_left, 0))
    if comm:
        pl.semaphore_wait(barrier, 3 + NY - 1 + NZ - 1 + NK - 1)
    halo = [
        remote(to_right, win.at[pl.ds(0, HROWS)], send_p.at[0], recv_p.at[0], right),
        remote(to_left, win.at[pl.ds(3 * HROWS, HROWS)], send_p.at[1], recv_p.at[1], left),
    ]
    start_all(halo)
    if not comm:
        win[pl.ds(0, HROWS), :] = to_right[...]
        win[pl.ds(3 * HROWS, HROWS), :] = to_left[...]
    pack_piece(feat_ref, cot_ref, (3, 0), 0, into(win, HROWS))
    pack_piece(feat_ref, cot_ref, (1, 2), HALF, into(win, 2 * HROWS))

    gain = gain_ref[...]
    shift = shift_ref[...]
    wq, wk, wv = (qkv_ref[:, e * D : (e + 1) * D] for e in range(3))
    wo = out_ref[...]
    scale = HEAD ** (-0.5)

    def project(first, rows):
        at = pl.ds(first, rows)
        packed = win[at, :]
        f = jnp.concatenate([packed[:, :128], packed[:, 256:320]], axis=1)
        c = jnp.concatenate([packed[:, 128:256], packed[:, 320:384]], axis=1)
        centred = f - jnp.sum(f, axis=1, keepdims=True) * (1.0 / D)
        inverse = lax.rsqrt(jnp.sum(centred * centred, axis=1, keepdims=True) * (1.0 / D) + EPSILON)
        standard = centred * inverse
        hidden = standard * gain + shift
        cot[at, :] = c
        unit[at, :] = standard
        inv[at, :] = inverse
        hid[at, :] = hidden
        que[at, :] = nn(hidden, wq) * scale
        key[at, :] = nn(hidden, wk)
        val[at, :] = nn(hidden, wv)
        gmx[at, :] = nt(c, wo)

    project(HROWS, 2 * HROWS)
    bias_strips(table_ref, perm_ref, mask_ref, turned, strip)
    wait_all(halo)
    project(0, HROWS)
    project(3 * HROWS, HROWS)

    mixtures, grad_q, grad_k, grad_v = [], [], [], []
    for w in range(PW):
        own = pl.ds(w * ROWS, ROWS)
        q_w, k_w, v_w, g_w = que[own, :], key[own, :], val[own, :], gmx[own, :]
        for h in range(HEADS):
            keep = head_lane(h, GROUP)
            for x in range(WLON):
                at = pl.ds(x * BLOCK + h * GROUP, GROUP)
                qs[at, :] = jnp.where(keep, q_w[x * GROUP : (x + 1) * GROUP], 0.0)
                gs[at, :] = jnp.where(keep, g_w[x * GROUP : (x + 1) * GROUP], 0.0)
        scores[...] = nt(qs[...], k_w)
        dattn[...] = nt(gs[...], v_w)
        band = strip[w]
        dband = jnp.zeros((BLOCK, STRIP), F32)
        for x in range(WLON):
            at = pl.ds(x * BLOCK, BLOCK)
            move = (WLON - 1 - x) * GROUP
            bias = band if move == 0 else pltpu.roll(band, STRIP - move, 1)
            s = scores[at, :] + bias[:, :ROWS]
            e = jnp.exp(s - jnp.max(s, axis=1, keepdims=True))
            a = e * (1.0 / jnp.sum(e, axis=1, keepdims=True))
            da = dattn[at, :]
            ds = a * (da - jnp.sum(a * da, axis=1, keepdims=True))
            scores[at, :] = a
            dattn[at, :] = ds
            wide = jnp.concatenate([ds, jnp.zeros((BLOCK, STRIP - ROWS), F32)], axis=1)
            dband = dband + (wide if move == 0 else pltpu.roll(wide, move, 1))
        turned[:, :BLOCK] = dband.T
        for n in range(POS):
            row = (n // WLAT) * 8 + n % WLAT
            lanes[pl.ds(w * 24, 24), n * 128 : n * 128 + 128] = turned[pl.ds(row, 24, stride=GROUP), :]
        if w == PW - 1:
            perm = perm_ref[...]
            sums = sum(nn(part, perm, None) for part in split(lanes[...], 2))
            for t in range(7):
                bsend[t] = sums[:, t * 128 : (t + 1) * 128]
            bsend[7] = jnp.zeros((48, 128), F32)
            step_b = (NZ, z, at_z, lambda o: bsend.at[o], brecv, send_b, recv_b)
            exchange(*step_b)
        att = scores[...]
        ds = dattn[...]
        grad_k.append(tn(ds, qs[...]))
        grad_v.append(tn(att, gs[...]))
        for source, other, sink in ((att, v_w, mixtures), (ds, k_w, grad_q)):
            qs[...] = nn(source, other)
            pieces = []
            for x in range(WLON):
                both = jnp.zeros((GROUP, D), F32)
                for h in range(HEADS):
                    both = jnp.where(
                        head_lane(h, GROUP), qs[pl.ds(x * BLOCK + h * GROUP, GROUP), :], both
                    )
                pieces.append(both)
            sink.append(jnp.concatenate(pieces, axis=0))

    mixture = jnp.concatenate(mixtures, axis=0)
    dq = jnp.concatenate(grad_q, axis=0) * scale
    dk = jnp.concatenate(grad_k, axis=0)
    dv = jnp.concatenate(grad_v, axis=0)

    hidden = hid[...]
    gq, gk, gv = tn(hidden, dq), tn(hidden, dk), tn(hidden, dv)
    go = tn(mixture, cot[...])
    columns = [
        gq[:, :128], gk[:, :128], gv[:, :128], go[:, :128],
        jnp.concatenate([gq[:, 128:], gk[:, 128:]], axis=1),
        jnp.concatenate([gv[:, 128:], go[:, 128:]], axis=1),
    ]
    for l in range(LAT):
        for g in range(6):
            wsend[l % 2, l // 2, pl.ds(g * 12, 12), :] = columns[g][l * 12 : (l + 1) * 12]
    swap = [remote(wsend.at[1 - core], crecv, send_c.at[0], recv_c.at[0], partner)]
    start_all(swap)

    gh = nt(dq, wq) + nt(dk, wk) + nt(dv, wv)
    standard = unit[...]
    ggain = jnp.sum(gh * standard, axis=0, keepdims=True)
    gshift = jnp.sum(gh, axis=0, keepdims=True)
    nsend[...] = jnp.concatenate(
        [
            ggain[:, :128], gshift[:, :128],
            jnp.concatenate([ggain[:, 128:], gshift[:, 128:]], axis=1),
            jnp.zeros((5, 128), F32),
        ],
        axis=0,
    )
    swap.append(remote(nsend, nrecv, send_c.at[1], recv_c.at[1], partner))
    start_all(swap[1:])
    gu = gh * gain
    mean_gu = jnp.sum(gu, axis=1, keepdims=True) * (1.0 / D)
    mean_uu = jnp.sum(gu * standard, axis=1, keepdims=True) * (1.0 / D)
    grad_ref[...] = cot[...] + inv[...] * (gu - mean_gu - standard * mean_uu)
    backs = [
        remote(grad_ref.at[pl.ds(0, HROWS)], piece.at[0], send_p.at[2], recv_p.at[2], left),
        remote(grad_ref.at[pl.ds(3 * HROWS, HROWS)], piece.at[1], send_p.at[3], recv_p.at[3], right),
    ]
    start_all(backs)
    if not comm:
        gathered[...] = bsend[...]
        hrecv[:, 0:72, :] = wsend[0]
        csum[:, 0:72, :] = wsend[1]
        hrecv[0, 72:80, :] = nsend[...]
        return

    step_y = (NY, y, at_y, lambda o: ypart, yrecv, send_y, recv_y)
    step_g = (NZ, z, at_z, lambda o: gathered.at[z], gathered, send_g, recv_g)
    step_h = (NK, k, at_k, lambda o: csum.at[o], hrecv, send_h, recv_h)
    step_z = (NZ, z, at_z, lambda o: zsend.at[o], zrecv, send_z, recv_z)
    step_l = (NY, y, at_y, lambda o: ysend, last, send_l, recv_l)

    wait_all(swap)
    both = nsend[...] + nrecv[...]
    for o in range(NK):
        csum[o, 0:72, :] = wsend[core, o] + crecv[o]
        csum[o, 72:80, :] = both
    exchange(*step_h)
    hrecv[k] = csum[k]

    brecv[z] = bsend[z]
    finish(*step_b)
    ypart[...] = total(brecv, NZ)
    exchange(*step_y)
    yrecv[y] = ypart[...]

    finish(*step_h)
    block = total(hrecv, NK)
    norm = block[72:75]
    lane = lax.broadcasted_iota(jnp.int32, (12, 128), 1)
    for t in range(NZ):
        main = block[(t // 2) * 12 : (t // 2) * 12 + 12]
        if t % 2:
            extra = block[48 + (t // 4) * 12 : 60 + (t // 4) * 12]
            tail = pltpu.roll(extra, 32 if (t // 2) % 2 == 0 else 96, 1)
            main = jnp.where(lane < 32, pltpu.roll(main, 32, 1), tail)
        zsend[t, 0:12, :] = main
        zsend[t, 12:15, :] = norm
        zsend[t, 15:16, :] = jnp.zeros((1, 128), F32)
    exchange(*step_z)
    zrecv[z] = zsend[z]

    finish(*step_y)
    gathered[z] = total(yrecv, NY)
    exchange(*step_g)

    finish(*step_z)
    ysend[...] = total(zrecv, NZ)
    exchange(*step_l)
    last[y] = ysend[...]

    wait_all(backs)
    finish(*step_g)
    finish(*step_l)


def main_call(comm, operands):
    vmem = pl.BlockSpec(memory_space=pltpu.VMEM)
    dma = pltpu.SemaphoreType.DMA
    sems = []
    for n in (4, 2, NK, NZ, NY, NZ, NZ, NY):
        sems += [dma((n,)), dma((n,))]

    def buf(*shape):
        return pltpu.VMEM(shape, F32)

    full = buf(PW * ROWS, D)
    wsend, csum, hrecv = buf(2, NK, 72, 128), buf(NK, 80, 128), buf(NK, 80, 128)
    params = dict(vmem_limit_bytes=VLIM)
    if comm:
        params.update(collective_id=0, has_side_effects=True)
    return pl.pallas_call(
        functools.partial(main_kernel, comm),
        out_shape=(
            jax.ShapeDtypeStruct((PW * ROWS, D), F32),
            jax.ShapeDtypeStruct((PW, HROWS, D), F32),
            jax.ShapeDtypeStruct((NZ, 48, 128), F32),
            jax.ShapeDtypeStruct((NY, 16, 128), F32),
        ),
        in_specs=[vmem] * 9,
        out_specs=(vmem,) * 4,
        scratch_shapes=[
            buf(PW * ROWS, 2 * D), buf(HROWS, 2 * D), buf(HROWS, 2 * D),
            full, full, full, buf(PW * ROWS, 1), full, full, full, full,
            buf(PW, BLOCK, STRIP), buf(STRIP, 128),
            buf(STACK, D), buf(STACK, D), buf(STACK, ROWS), buf(STACK, ROWS),
            buf(PW, BLOCK, STRIP), buf(48, POS * 128),
            wsend, buf(8, 128), buf(NZ, 48, 128), buf(NK, 72, 128), buf(8, 128), csum, hrecv,
            buf(NZ, 48, 128), buf(48, 128), buf(NY, 48, 128),
            buf(NZ, 16, 128), buf(NZ, 16, 128), buf(16, 128),
        ] + sems,
        compiler_params=pltpu.CompilerParams(**params),
        name="window_block",
    )(*operands)


def unpack_kernel(grad_ref, piece, gathered, last, feat_ref, weight_ref, bias_ref, norm_ref):
    y = lax.rem(lax.axis_index("lon"), NY)
    for x in range(HALF):
        for c, slabs in ((0, (3, 0)), (1, (1, 2))):
            for i, slab in enumerate(slabs):
                row = x * GROUP + i * 8
                own = grad_ref[pl.ds((1 + c) * HROWS + row, 8), :]
                far = piece[c, pl.ds(row, 8), :]
                west, east = (own, far) if c == 0 else (far, own)
                feat_ref[:, x, slab, :] = west[:WLAT]
                feat_ref[:, HALF + x, slab, :] = east[:WLAT]
    for h in range(HEADS):
        main = gathered[h]
        rem = gathered[6]
        rem = rem if h == 0 else pltpu.roll(rem, 128 - 16 * h, 1)
        for c in range(PW):
            bias_ref[h, :, c, 0:128] = main[c * 24 : c * 24 + LONREL]
            bias_ref[h, :, c, 128:144] = rem[c * 24 : c * 24 + LONREL, :16]
    both = functools.reduce(lambda a, b: a + b, [last[s] for s in range(NY)]) * (1.0 / 384.0)
    rows = both[0:12]
    mine = rows[:, 0:24]
    for t in range(1, NY):
        mine = jnp.where(y == t, pltpu.roll(rows, 128 - 24 * t, 1)[:, 0:24], mine)
    weight_ref[...] = mine
    norm_ref[0:1, 0:128] = both[12:13]
    norm_ref[1:2, 0:128] = both[13:14]
    norm_ref[0:1, 128:192] = both[14:15, 0:64]
    norm_ref[1:2, 128:192] = both[14:15, 64:128]


def unpack(operands):
    vmem = pl.BlockSpec(memory_space=pltpu.VMEM)
    return pl.pallas_call(
        unpack_kernel,
        out_shape=(
            jax.ShapeDtypeStruct((WLAT, WLON, 4, D), F32),
            jax.ShapeDtypeStruct((12, 24), F32),
            jax.ShapeDtypeStruct((HEADS, LONREL, PW, PAIRS), F32),
            jax.ShapeDtypeStruct((2, D), F32),
        ),
        in_specs=[vmem] * 4,
        out_specs=(vmem,) * 4,
        compiler_params=pltpu.CompilerParams(vmem_limit_bytes=8 * 1024 * 1024),
        name="unpack",
    )(*operands)


def operands_of(features, cotangent, norm_gain, norm_shift, qkv_weight, out_weight, bias_table):
    return (
        features.transpose(1, 2, 0, 3),
        cotangent.transpose(1, 2, 0, 3),
        norm_gain.reshape(1, D),
        norm_shift.reshape(1, D),
        qkv_weight,
        out_weight,
        bias_table.reshape(PW, HEADS, LONREL, PAIRS).transpose(1, 2, 0, 3),
        jnp.asarray(permutation(), jnp.bfloat16),
        jnp.asarray(mask_strips()),
    )


def shards(*args):
    grad_features, grad_weights, grad_bias, grad_norm = unpack(main_call(True, operands_of(*args)))
    return (
        grad_features.transpose(2, 0, 1, 3),
        grad_weights,
        grad_bias.transpose(2, 0, 1, 3).reshape(1, PW, HEADS, LONREL, PAIRS),
        grad_norm,
    )


def solution(mesh):
    placed = (
        P(None, "lat", "lon", None),
        P(None, "lat", "lon", None),
        P(),
        P(),
        P(),
        P(),
        P("lat", None, None, None, None),
    )
    return jax.shard_map(
        shards,
        mesh=mesh,
        in_specs=placed,
        out_specs=(
            P(None, "lat", "lon", None),
            P("lat", "lon"),
            P("lat", None, None, None, None),
            P(),
        ),
        check_vma=False,
    )
```

```python
import functools

import jax
import jax.numpy as jnp
import numpy as np
from jax import lax
from jax.experimental import pallas as pl
from jax.experimental.pallas import tpu as pltpu
from jax.sharding import PartitionSpec as P

D = 192
HEADS = 6
HEAD = 32
WLAT = 6
WLON = 12
HALF = WLON // 2
PW = 2
LONREL = 23
PAIRS = 144
EPSILON = 1e-05

GROUP = 16
ROWS = WLON * GROUP
HROWS = HALF * GROUP
PSTACK = 2 * ROWS
PIECES = 2 * HALF
BF16 = jnp.bfloat16
BLOCK = HEADS * GROUP
STRIP = 24 * GROUP
POS = 12
TABW = 896
NEG = -1e30
PAIRS_OF_HEADS = 3
LANES = 2 * HEAD
F32 = jnp.float32
HIGH = lax.Precision.HIGH
MESH = pl.DeviceIdType.MESH
LAT = 16
NK = 8
NZ = 8
NY = 4
VLIM = 32 * 1024 * 1024


def permutation():
    out = np.zeros((POS * 128, TABW), np.float32)
    for n in range(POS):
        j, b = divmod(n, WLAT)
        for h in range(HEADS):
            for i in range(2):
                for a in range(WLAT):
                    p = ((i * 2 + j) * WLAT + a) * WLAT + b
                    col = h * 128 + p if p < 128 else 768 + h * 16 + p - 128
                    out[n * 128 + h * GROUP + i * 8 + a, col] = 1.0
    return out


def nn(a, b, precision=HIGH):
    return lax.dot_general(a, b, (((1,), (0,)), ((), ())), precision=precision, preferred_element_type=F32)


def nt(a, b, precision=HIGH):
    return lax.dot_general(a, b, (((1,), (1,)), ((), ())), precision=precision, preferred_element_type=F32)


def tn(a, b, precision=HIGH):
    return lax.dot_general(a, b, (((0,), (0,)), ((), ())), precision=precision, preferred_element_type=F32)


def split(x, terms):
    parts = []
    for _ in range(terms):
        part = x.astype(jnp.bfloat16)
        parts.append(part)
        x = x - part.astype(F32)
    return parts


def strip_mask(c):
    lane = lax.broadcasted_iota(jnp.int32, (BLOCK, STRIP), 1)
    row = lax.broadcasted_iota(jnp.int32, (BLOCK, STRIP), 0)
    shut = (lane & 7) >= WLAT
    if c == 0:
        shut = shut | (((lane >> 3) & 1) != ((row >> 3) & 1))
    return jnp.where(shut, NEG, 0.0)


def bias_strips(table_ref, perm_ref, turned, strip):
    zero_row = jnp.zeros((1, 128), F32)
    rem_row = jnp.zeros((1, 16), F32)
    mains, rems = [], []
    for c in range(PW):
        main, rem = [], []
        for h in range(HEADS):
            t = table_ref[h, :, c, :]
            main.append(jnp.concatenate([t[:, :128], zero_row], axis=0))
            rem.append(jnp.concatenate([t[:, 128:], rem_row], axis=0))
        rem.append(jnp.zeros((24, 32), F32))
        mains.append(jnp.concatenate(main, axis=1))
        rems.append(jnp.concatenate(rem, axis=1))
    table = jnp.concatenate(
        [jnp.concatenate(mains, axis=0), jnp.concatenate(rems, axis=0)], axis=1
    )
    perm = perm_ref[...]
    spread = sum(nt(part, perm, None) for part in split(table, 3))
    for c in range(PW):
        for n in range(POS):
            row = (n // WLAT) * 8 + n % WLAT
            turned[pl.ds(row, 24, stride=GROUP), :] = spread[c * 24 : c * 24 + 24, n * 128 : n * 128 + 128]
        for n in (6, 7, 14, 15):
            turned[pl.ds(n, 24, stride=GROUP), :] = jnp.zeros((24, 128), F32)
        strip[c] = turned[...].T[:BLOCK, :] + strip_mask(c)


def parity_lanes(width):
    lane = lax.broadcasted_iota(jnp.int32, (1, width), 1)
    second = ((lane >> 5) & 1).astype(F32)
    return (1.0 - second).astype(BF16), second.astype(BF16)


def pair_rows(high, low, p):
    lanes = slice(p * LANES, (p + 1) * LANES)
    joined = jnp.concatenate([high[:, lanes], low[:, lanes], high[:, lanes]], axis=1)
    first, second = parity_lanes(3 * LANES)
    cells = joined.reshape(WLON, GROUP, 3 * LANES)
    return jnp.concatenate([cells * first, cells * second], axis=1).reshape(PSTACK, 3 * LANES)


def pair_cols(high, low, p):
    lanes = slice(p * LANES, (p + 1) * LANES)
    return jnp.concatenate([high[:, lanes], high[:, lanes], low[:, lanes]], axis=1)


def pick_heads(value):
    cells = value.reshape(WLON, 2 * GROUP, LANES)
    lane = lax.broadcasted_iota(jnp.int32, (WLON, GROUP, LANES), 2)
    return jnp.where(lane < HEAD, cells[:, :GROUP], cells[:, GROUP:]).reshape(ROWS, LANES)


def main_kernel(
    comm,
    feat_hbm, cot_hbm, gain_hbm, shift_hbm, qkv_hbm, out_hbm, table_hbm, perm_hbm,
    *refs,
):
    if not comm:
        spare, refs = refs[4], refs[:4] + refs[5:]
    (
        grad_ref, piece, gathered, last,
        feat_ref, cot_ref, gain_ref, shift_ref, qkv_ref, out_ref, table_ref, perm_ref, load_sem,
        halo_out, halo_in, win, back_out, unit, cot, inv, hid,
        qh, ql, kh, kl, vh, vl, gh_, gl_,
        strip, turned, qst, gst, scores, dattn, ah, al, dh, dl, lanes,
        wsend, xsend, nsend, bsend, wcore, xcore, ncore, wsum, xsum, wrecv, xrecv,
        brecv, ypart, yrecv, zsend, zrecv, ysend,
        send_p, recv_p, send_c, recv_c, send_h, recv_h, send_x, recv_x, send_b, recv_b,
        send_y, recv_y, send_g, recv_g, send_z, recv_z, send_l, recv_l,
    ) = refs
    loads = [
        pltpu.make_async_copy(src, dst, load_sem.at[i])
        for i, (src, dst) in enumerate(
            (
                (feat_hbm, feat_ref), (cot_hbm, cot_ref), (gain_hbm, gain_ref), (shift_hbm, shift_ref),
                (qkv_hbm, qkv_ref), (out_hbm, out_ref), (table_hbm, table_ref), (perm_hbm, perm_ref),
            )
        )
    ]
    for load in loads:
        load.start()
    if comm:
        lat, lon = lax.axis_index("lat"), lax.axis_index("lon")
    else:
        lat, lon = jnp.int32(0), jnp.int32(0)
    count = NZ * NY
    z, y = lon // NY, lax.rem(lon, NY)
    k, core = lat // 2, lax.rem(lat, 2)
    right, left = {"lon": lax.rem(lon + 1, count)}, {"lon": lax.rem(lon + count - 1, count)}
    partner = {"lat": k * 2 + 1 - core}

    def at_k(i):
        return {"lat": lax.rem(k + i, NK) * 2 + core}

    def at_z(i):
        return {"lon": lax.rem(z + i, NZ) * NY + y}

    def at_y(i):
        return {"lon": z * NY + lax.rem(y + i, NY)}

    def remote(src, dst, send, recv, device):
        return pltpu.make_async_remote_copy(
            src_ref=src, dst_ref=dst, send_sem=send, recv_sem=recv, device_id=device, device_id_type=MESH
        )

    def start_all(copies):
        for copy in copies if comm else ():
            copy.start()

    def wait_all(copies):
        for copy in copies if comm else ():
            copy.wait()

    def exchange(n, mine, where, src, dst, send, recv):
        def start(i, carry):
            other = lax.rem(mine + i, n)
            remote(src(other), dst.at[mine], send.at[i], recv.at[mine], where(i)).start()
            return carry

        if comm:
            lax.fori_loop(1, n, start, 0)

    def finish(n, mine, where, src, dst, send, recv):
        def done(i, carry):
            other = lax.rem(mine + i, n)
            copy = remote(src(other), dst.at[other], send.at[i], recv.at[other], where(i))
            copy.wait_send()
            copy.wait_recv()
            return carry

        if comm:
            lax.fori_loop(1, n, done, 0)

    def total(ref, n):
        return functools.reduce(lambda a, b: a + b, [ref[s] for s in range(n)])

    if comm:
        barrier = pltpu.get_barrier_semaphore()

        def greet(where):
            def step(i, carry):
                pl.semaphore_signal(barrier, inc=1, device_id=where(i), device_id_type=MESH)
                return carry

            return step

        lax.fori_loop(1, NY, greet(at_y), 0)
        lax.fori_loop(1, NZ, greet(at_z), 0)
        lax.fori_loop(1, NK, greet(at_k), 0)
        for device in (left, right, partner):
            pl.semaphore_signal(barrier, inc=1, device_id=device, device_id_type=MESH)

    def tiles(slabs, first):
        for x in range(HALF):
            for i, slab in enumerate(slabs):
                f = feat_ref[:, first + x, slab, :]
                c = cot_ref[:, first + x, slab, :]
                mixed = jnp.concatenate([f[:, 128:], c[:, 128:]], axis=1)
                yield x * 2 + i, (f[:, :128], mixed, c[:, :128])

    loads[0].wait()
    loads[1].wait()
    for d, (slabs, first) in enumerate((((3, 0), HALF), ((1, 2), 0))):
        for g, parts in tiles(slabs, first):
            for t in range(3):
                halo_out[d, t * PIECES + g] = parts[t]
    if comm:
        pl.semaphore_wait(barrier, 3 + NY - 1 + NZ - 1 + NK - 1)
    cuts = (pl.ds(0, 2 * PIECES), pl.ds(2 * PIECES, PIECES))
    halo = [
        [
            remote(halo_out.at[d, cut], halo_in.at[d, cut], send_p.at[2 * e + d], recv_p.at[2 * e + d], (right, left)[d])
            for d in range(2)
        ]
        for e, cut in enumerate(cuts)
    ]
    start_all(halo[0])
    start_all(halo[1])
    gap = jnp.zeros((2, 128), F32)
    for base, slabs, first in ((HROWS, (3, 0), 0), (2 * HROWS, (1, 2), HALF)):
        for g, parts in tiles(slabs, first):
            for t in range(3):
                win[t, pl.ds(base + g * 8, 8), :] = jnp.concatenate([parts[t], gap], axis=0)

    def arrived(which):
        for d, base in ((0, 0), (1, 3 * HROWS)):
            for t in which:
                for g in range(PIECES):
                    source = halo_in if comm else halo_out
                    win[t, pl.ds(base + g * 8, 8), :] = jnp.concatenate(
                        [source[d, t * PIECES + g], gap], axis=0
                    )

    for load in loads[2:6]:
        load.wait()
    gain = gain_ref[...]
    shift = shift_ref[...]
    wq, wk, wv = (qkv_ref[:, e * D : (e + 1) * D] for e in range(3))
    wo = out_ref[...]
    scale = HEAD ** (-0.5)

    def keep(at, value, high, low):
        high[at, :], low[at, :] = split(value, 2)

    def project_features(first, rows):
        at = pl.ds(first, rows)
        f = jnp.concatenate([win[0, at, :], win[1, at, :][:, :64]], axis=1)
        centred = f - jnp.sum(f, axis=1, keepdims=True) * (1.0 / D)
        inverse = lax.rsqrt(jnp.sum(centred * centred, axis=1, keepdims=True) * (1.0 / D) + EPSILON)
        standard = centred * inverse
        hidden = standard * gain + shift
        unit[at, :] = standard
        inv[at, :] = inverse
        hid[at, :] = hidden
        keep(at, nn(hidden, wq) * scale, qh, ql)
        keep(at, nn(hidden, wk), kh, kl)
        keep(at, nn(hidden, wv), vh, vl)

    def project_cotangent(first, rows):
        at = pl.ds(first, rows)
        c = jnp.concatenate([win[2, at, :], win[1, at, :][:, 64:]], axis=1)
        cot[at, :] = c
        keep(at, nt(c, wo), gh_, gl_)

    project_features(HROWS, 2 * HROWS)
    project_cotangent(HROWS, 2 * HROWS)
    loads[6].wait()
    loads[7].wait()
    bias_strips(table_ref, perm_ref, turned, strip)

    wait_all(halo[0])
    arrived((0, 1))
    project_features(0, HROWS)
    project_features(3 * HROWS, HROWS)
    windows = [pl.ds(w * ROWS, ROWS) for w in range(PW)]
    for w, own in enumerate(windows):
        for p in range(PAIRS_OF_HEADS):
            rows = pair_rows(qh[own, :], ql[own, :], p)
            qst[w, p] = rows
            part = nt(rows, pair_cols(kh[own, :], kl[own, :], p), None)
            scores[w, :, p * 32 : p * 32 + 32, :] = part.reshape(WLON, 32, ROWS)

    wait_all(halo[1])
    arrived((2,))
    project_cotangent(0, HROWS)
    project_cotangent(3 * HROWS, HROWS)
    for w, own in enumerate(windows):
        for p in range(PAIRS_OF_HEADS):
            rows = pair_rows(gh_[own, :], gl_[own, :], p)
            gst[w, p] = rows
            part = nt(rows, pair_cols(vh[own, :], vl[own, :], p), None)
            dattn[w, :, p * 32 : p * 32 + 32, :] = part.reshape(WLON, 32, ROWS)

    for w in range(PW):
        band = strip[w]
        dband = jnp.zeros((BLOCK, STRIP), F32)
        for x in range(WLON):
            move = (WLON - 1 - x) * GROUP
            bias = band if move == 0 else pltpu.roll(band, STRIP - move, 1)
            s = scores[w, x] + bias[:, :ROWS]
            e = jnp.exp(s - jnp.max(s, axis=1, keepdims=True))
            a = e * (1.0 / jnp.sum(e, axis=1, keepdims=True))
            da = dattn[w, x]
            ds = a * (da - jnp.sum(a * da, axis=1, keepdims=True))
            ah[w, x], al[w, x] = split(a, 2)
            dh[w, x], dl[w, x] = split(ds, 2)
            wide = jnp.concatenate([ds, jnp.zeros((BLOCK, STRIP - ROWS), F32)], axis=1)
            dband = dband + (wide if move == 0 else pltpu.roll(wide, move, 1))
        turned[:, :BLOCK] = dband.T
        for n in range(POS):
            row = (n // WLAT) * 8 + n % WLAT
            lanes[pl.ds(w * 24, 24), n * 128 : n * 128 + 128] = turned[pl.ds(row, 24, stride=GROUP), :]

    def pair_of(ref, w, p):
        return ref[w, :, p * 32 : p * 32 + 32, :].reshape(PSTACK, ROWS)

    def applied(high, low, other_high, other_low):
        result = []
        for w, own in enumerate(windows):
            cols = []
            for p in range(PAIRS_OF_HEADS):
                at = slice(p * LANES, (p + 1) * LANES)
                oh = other_high[own, :][:, at]
                both = nn(pair_of(high, w, p), jnp.concatenate([oh, other_low[own, :][:, at]], axis=1), None)
                rest = nn(pair_of(low, w, p), oh, None)
                cols.append(pick_heads(both[:, :LANES] + both[:, LANES:] + rest))
            result.append(jnp.concatenate(cols, axis=1))
        return jnp.concatenate(result, axis=0)

    def gathered_keys(high, low, stack):
        result = []
        for w in range(PW):
            cols = []
            for p in range(PAIRS_OF_HEADS):
                rows = stack[w, p]
                both = tn(pair_of(high, w, p), rows[:, : 2 * LANES], None)
                rest = tn(pair_of(low, w, p), rows[:, :LANES], None)
                cols.append(both[:, :LANES] + both[:, LANES:] + rest)
            result.append(jnp.concatenate(cols, axis=1))
        return jnp.concatenate(result, axis=0)

    def cut(ref, one, two):
        columns = [
            one[:, :128], two[:, :128],
            jnp.concatenate([one[:, 128:], two[:, 128:]], axis=1),
        ]
        for l in range(LAT):
            for g in range(3):
                ref[l % 2, l // 2, pl.ds(g * 12, 12), :] = columns[g][l * 12 : (l + 1) * 12]

    mixture = applied(ah, al, vh, vl)
    dv = gathered_keys(ah, al, gst)
    hidden = hid[...]
    cut(wsend, tn(hidden, dv), tn(mixture, cot[...]))
    swap = [
        remote(wsend.at[1 - core], wcore, send_c.at[0], recv_c.at[0], partner),
        remote(xsend.at[1 - core], xcore, send_c.at[1], recv_c.at[1], partner),
        remote(nsend, ncore, send_c.at[2], recv_c.at[2], partner),
    ]
    start_all(swap[:1])

    perm = perm_ref[...]
    sums = sum(nn(part, perm, None) for part in split(lanes[...], 2))
    for t in range(7):
        bsend[t] = sums[:, t * 128 : (t + 1) * 128]
    bsend[7] = jnp.zeros((48, 128), F32)
    step_b = (NZ, z, at_z, lambda o: bsend.at[o], brecv, send_b, recv_b)
    exchange(*step_b)

    dq = applied(dh, dl, kh, kl) * scale
    step_h = (NK, k, at_k, lambda o: wsum.at[o], wrecv, send_h, recv_h)
    step_x = (NK, k, at_k, lambda o: xsum.at[o], xrecv, send_x, recv_x)
    wait_all(swap[:1])
    if comm:
        for o in range(NK):
            wsum[o] = wsend[core, o] + wcore[o]
        exchange(*step_h)
        wrecv[k] = wsum[k]

    dk = gathered_keys(dh, dl, qst)
    cut(xsend, tn(hidden, dq), tn(hidden, dk))
    start_all(swap[1:2])

    gh = nt(dq, wq) + nt(dk, wk) + nt(dv, wv)
    standard = unit[...]
    ggain = jnp.sum(gh * standard, axis=0, keepdims=True)
    gshift = jnp.sum(gh, axis=0, keepdims=True)
    nsend[...] = jnp.concatenate(
        [
            ggain[:, :128], gshift[:, :128],
            jnp.concatenate([ggain[:, 128:], gshift[:, 128:]], axis=1),
            jnp.zeros((1, 128), F32),
        ],
        axis=0,
    )
    start_all(swap[2:])
    wait_all(swap[1:])
    if comm:
        for o in range(NK):
            xsum[o, 0:36, :] = xsend[core, o] + xcore[o]
            xsum[o, 36:40, :] = nsend[...] + ncore[...]
        exchange(*step_x)
        xrecv[k] = xsum[k]

    gu = gh * gain
    mean_gu = jnp.sum(gu, axis=1, keepdims=True) * (1.0 / D)
    mean_uu = jnp.sum(gu * standard, axis=1, keepdims=True) * (1.0 / D)
    grad_ref[...] = cot[...] + inv[...] * (gu - mean_gu - standard * mean_uu)
    for d, base in ((0, 0), (1, 3 * HROWS)):
        for g in range(PIECES):
            back_out[d, g] = grad_ref[pl.ds(base + g * 8, WLAT), :]
    backs = [
        remote(back_out.at[d], piece.at[d], send_p.at[4 + d], recv_p.at[4 + d], (left, right)[d])
        for d in range(2)
    ]
    start_all(backs)
    if not comm:
        gathered[...] = bsend[...]
        spare[0] = wsend[...]
        spare[1] = xsend[...]
        last[0, 0:4, :] = nsend[...]
        return

    step_y = (NY, y, at_y, lambda o: ypart, yrecv, send_y, recv_y)
    step_g = (NZ, z, at_z, lambda o: gathered.at[z], gathered, send_g, recv_g)
    step_z = (NZ, z, at_z, lambda o: zsend.at[o], zrecv, send_z, recv_z)
    step_l = (NY, y, at_y, lambda o: ysend, last, send_l, recv_l)

    brecv[z] = bsend[z]
    finish(*step_b)
    ypart[...] = total(brecv, NZ)
    exchange(*step_y)
    yrecv[y] = ypart[...]

    finish(*step_h)
    block_vo = total(wrecv, NK)
    finish(*step_x)
    block_qk = total(xrecv, NK)
    norm = block_qk[36:39]
    lane = lax.broadcasted_iota(jnp.int32, (12, 128), 1)
    for t in range(NZ):
        block = block_qk if t < 4 else block_vo
        e = (t // 2) % 2
        main = block[e * 12 : e * 12 + 12]
        if t % 2:
            tail = pltpu.roll(block[24:36], 96 if e else 32, 1)
            main = jnp.where(lane < 32, pltpu.roll(main, 32, 1), tail)
        zsend[t, 0:12, :] = main
        zsend[t, 12:15, :] = norm
        zsend[t, 15:16, :] = jnp.zeros((1, 128), F32)
    exchange(*step_z)
    zrecv[z] = zsend[z]

    finish(*step_y)
    gathered[z] = total(yrecv, NY)
    exchange(*step_g)

    finish(*step_z)
    ysend[...] = total(zrecv, NZ)
    exchange(*step_l)
    last[y] = ysend[...]

    wait_all(backs)
    finish(*step_g)
    finish(*step_l)


def main_call(comm, operands):
    vmem = pl.BlockSpec(memory_space=pltpu.VMEM)
    hbm = pl.BlockSpec(memory_space=pltpu.HBM)
    dma = pltpu.SemaphoreType.DMA
    sems = []
    for n in (6, 3, NK, NK, NZ, NY, NZ, NZ, NY):
        sems += [dma((n,)), dma((n,))]

    def buf(*shape):
        return pltpu.VMEM(shape, F32)

    def half(*shape):
        return pltpu.VMEM(shape, BF16)

    full = buf(PW * ROWS, D)
    token = half(PW * ROWS, D)
    stack = half(PW, PAIRS_OF_HEADS, PSTACK, 3 * LANES)
    square = (PW, WLON, BLOCK, ROWS)
    outs = (
        jax.ShapeDtypeStruct((PW * ROWS, D), F32),
        jax.ShapeDtypeStruct((PW, PIECES, WLAT, D), F32),
        jax.ShapeDtypeStruct((NZ, 48, 128), F32),
        jax.ShapeDtypeStruct((NY, 16, 128), F32),
    )
    params = dict(vmem_limit_bytes=VLIM)
    if comm:
        params.update(collective_id=0, has_side_effects=True)
    else:
        outs += (jax.ShapeDtypeStruct((2, 2, NK, 36, 128), F32),)
    return pl.pallas_call(
        functools.partial(main_kernel, comm),
        out_shape=outs,
        in_specs=[hbm] * 8,
        out_specs=(vmem,) * len(outs),
        scratch_shapes=[pltpu.VMEM(t.shape, t.dtype) for t in operands] + [
            dma((8,)),
            buf(2, 3 * PIECES, WLAT, 128), buf(2, 3 * PIECES, WLAT, 128), buf(3, PW * ROWS, 128),
            buf(2, PIECES, WLAT, D),
            full, full, buf(PW * ROWS, 1), full,
            token, token, token, token, token, token, token, token,
            buf(PW, BLOCK, STRIP), buf(STRIP, 128), stack, stack, buf(*square), buf(*square),
            half(*square), half(*square), half(*square), half(*square), buf(48, POS * 128),
            buf(2, NK, 36, 128), buf(2, NK, 36, 128), buf(4, 128), buf(NZ, 48, 128),
            buf(NK, 36, 128), buf(NK, 36, 128), buf(4, 128),
            buf(NK, 36, 128), buf(NK, 40, 128), buf(NK, 36, 128), buf(NK, 40, 128),
            buf(NZ, 48, 128), buf(48, 128), buf(NY, 48, 128),
            buf(NZ, 16, 128), buf(NZ, 16, 128), buf(16, 128),
        ] + sems,
        compiler_params=pltpu.CompilerParams(**params),
        name="window_block",
    )(*(pltpu.with_memory_space_constraint(t, pltpu.HBM) for t in operands))


def unpack_kernel(grad_ref, piece, gathered, last, feat_ref, weight_ref, bias_ref, norm_ref):
    y = lax.rem(lax.axis_index("lon"), NY)
    for x in range(HALF):
        for c, slabs in ((0, (3, 0)), (1, (1, 2))):
            for i, slab in enumerate(slabs):
                row = x * GROUP + i * 8
                own = grad_ref[pl.ds((1 + c) * HROWS + row, 8), :]
                own, far = own[:WLAT], piece[c, x * 2 + i]
                west, east = (own, far) if c == 0 else (far, own)
                feat_ref[:, x, slab, :] = west
                feat_ref[:, HALF + x, slab, :] = east
    for h in range(HEADS):
        main = gathered[h]
        rem = gathered[6]
        rem = rem if h == 0 else pltpu.roll(rem, 128 - 16 * h, 1)
        for c in range(PW):
            bias_ref[h, :, c, 0:128] = main[c * 24 : c * 24 + LONREL]
            bias_ref[h, :, c, 128:144] = rem[c * 24 : c * 24 + LONREL, :16]
    both = functools.reduce(lambda a, b: a + b, [last[s] for s in range(NY)]) * (1.0 / 384.0)
    rows = both[0:12]
    mine = rows[:, 0:24]
    for t in range(1, NY):
        mine = jnp.where(y == t, pltpu.roll(rows, 128 - 24 * t, 1)[:, 0:24], mine)
    weight_ref[...] = mine
    norm_ref[0:1, 0:128] = both[12:13]
    norm_ref[1:2, 0:128] = both[13:14]
    norm_ref[0:1, 128:192] = both[14:15, 0:64]
    norm_ref[1:2, 128:192] = both[14:15, 64:128]


def unpack(operands):
    vmem = pl.BlockSpec(memory_space=pltpu.VMEM)
    return pl.pallas_call(
        unpack_kernel,
        out_shape=(
            jax.ShapeDtypeStruct((WLAT, WLON, 4, D), F32),
            jax.ShapeDtypeStruct((12, 24), F32),
            jax.ShapeDtypeStruct((HEADS, LONREL, PW, PAIRS), F32),
            jax.ShapeDtypeStruct((2, D), F32),
        ),
        in_specs=[vmem] * 4,
        out_specs=(vmem,) * 4,
        compiler_params=pltpu.CompilerParams(vmem_limit_bytes=8 * 1024 * 1024),
        name="unpack",
    )(*operands)


def operands_of(features, cotangent, norm_gain, norm_shift, qkv_weight, out_weight, bias_table):
    return (
        features.transpose(1, 2, 0, 3),
        cotangent.transpose(1, 2, 0, 3),
        norm_gain.reshape(1, D),
        norm_shift.reshape(1, D),
        qkv_weight,
        out_weight,
        bias_table.reshape(PW, HEADS, LONREL, PAIRS).transpose(1, 2, 0, 3),
        jnp.asarray(permutation(), jnp.bfloat16),
    )


def shards(*args):
    grad_features, grad_weights, grad_bias, grad_norm = unpack(main_call(True, operands_of(*args)))
    return (
        grad_features.transpose(2, 0, 1, 3),
        grad_weights,
        grad_bias.transpose(2, 0, 1, 3).reshape(1, PW, HEADS, LONREL, PAIRS),
        grad_norm,
    )


def solution(mesh):
    placed = (
        P(None, "lat", "lon", None),
        P(None, "lat", "lon", None),
        P(),
        P(),
        P(),
        P(),
        P("lat", None, None, None, None),
    )
    return jax.shard_map(
        shards,
        mesh=mesh,
        in_specs=placed,
        out_specs=(
            P(None, "lat", "lon", None),
            P("lat", "lon"),
            P("lat", None, None, None, None),
            P(),
        ),
        check_vma=False,
    )
```

```python
import functools

import jax
import jax.numpy as jnp
import numpy as np
from jax import lax
from jax.experimental import pallas as pl
from jax.experimental.pallas import tpu as pltpu
from jax.sharding import PartitionSpec as P

D = 192
HEADS = 6
HEAD = 32
WLAT = 6
WLON = 12
HALF = WLON // 2
PW = 2
LONREL = 23
PAIRS = 144
EPSILON = 1e-05

GROUP = 16
ROWS = WLON * GROUP
HROWS = HALF * GROUP
PSTACK = 2 * ROWS
PIECES = 2 * HALF
BF16 = jnp.bfloat16
BLOCK = HEADS * GROUP
STRIP = 24 * GROUP
POS = 12
TABW = 896
NEG = -1e30
FAR_FIRST = {4: (2, 1, 3), 8: (4, 3, 5, 2, 6, 1, 7)}
PAIRS_OF_HEADS = 3
LANES = 2 * HEAD
F32 = jnp.float32
HIGH = lax.Precision.HIGH
MESH = pl.DeviceIdType.MESH
LAT = 16
NK = 8
NZ = 8
NY = 4
VLIM = 32 * 1024 * 1024


def permutation():
    out = np.zeros((POS * 128, TABW), np.float32)
    for n in range(POS):
        j, b = divmod(n, WLAT)
        for h in range(HEADS):
            for i in range(2):
                for a in range(WLAT):
                    p = ((i * 2 + j) * WLAT + a) * WLAT + b
                    col = h * 128 + p if p < 128 else 768 + h * 16 + p - 128
                    out[n * 128 + h * GROUP + i * 8 + a, col] = 1.0
    return out


def nn(a, b, precision=HIGH):
    return lax.dot_general(a, b, (((1,), (0,)), ((), ())), precision=precision, preferred_element_type=F32)


def nt(a, b, precision=HIGH):
    return lax.dot_general(a, b, (((1,), (1,)), ((), ())), precision=precision, preferred_element_type=F32)


def tn(a, b, precision=HIGH):
    return lax.dot_general(a, b, (((0,), (0,)), ((), ())), precision=precision, preferred_element_type=F32)


def split(x, terms):
    parts = []
    for _ in range(terms):
        part = x.astype(jnp.bfloat16)
        parts.append(part)
        x = x - part.astype(F32)
    return parts


def strip_mask(c):
    lane = lax.broadcasted_iota(jnp.int32, (BLOCK, STRIP), 1)
    row = lax.broadcasted_iota(jnp.int32, (BLOCK, STRIP), 0)
    shut = (lane & 7) >= WLAT
    if c == 0:
        shut = shut | (((lane >> 3) & 1) != ((row >> 3) & 1))
    return jnp.where(shut, NEG, 0.0)


def bias_strips(table_ref, perm_ref, turned, strip):
    zero_row = jnp.zeros((1, 128), F32)
    rem_row = jnp.zeros((1, 16), F32)
    mains, rems = [], []
    for c in range(PW):
        main, rem = [], []
        for h in range(HEADS):
            t = table_ref[h, :, c, :]
            main.append(jnp.concatenate([t[:, :128], zero_row], axis=0))
            rem.append(jnp.concatenate([t[:, 128:], rem_row], axis=0))
        rem.append(jnp.zeros((24, 32), F32))
        mains.append(jnp.concatenate(main, axis=1))
        rems.append(jnp.concatenate(rem, axis=1))
    table = jnp.concatenate(
        [jnp.concatenate(mains, axis=0), jnp.concatenate(rems, axis=0)], axis=1
    )
    perm = perm_ref[...]
    spread = sum(nt(part, perm, None) for part in split(table, 3))
    for c in range(PW):
        for n in range(POS):
            row = (n // WLAT) * 8 + n % WLAT
            turned[pl.ds(row, 24, stride=GROUP), :] = spread[c * 24 : c * 24 + 24, n * 128 : n * 128 + 128]
        for n in (6, 7, 14, 15):
            turned[pl.ds(n, 24, stride=GROUP), :] = jnp.zeros((24, 128), F32)
        band = turned[...].T[:BLOCK, :] + strip_mask(c)
        for x in range(WLON):
            move = (WLON - 1 - x) * GROUP
            strip[c, x] = (band if move == 0 else pltpu.roll(band, STRIP - move, 1))[:, :ROWS]


def parity_lanes(width):
    lane = lax.broadcasted_iota(jnp.int32, (1, width), 1)
    second = ((lane >> 5) & 1).astype(F32)
    return (1.0 - second).astype(BF16), second.astype(BF16)


def pair_rows(high, low, p):
    lanes = slice(p * LANES, (p + 1) * LANES)
    joined = jnp.concatenate([high[:, lanes], low[:, lanes], high[:, lanes]], axis=1)
    first, second = parity_lanes(3 * LANES)
    cells = joined.reshape(WLON, GROUP, 3 * LANES)
    return jnp.concatenate([cells * first, cells * second], axis=1).reshape(PSTACK, 3 * LANES)


def pair_cols(high, low, p):
    lanes = slice(p * LANES, (p + 1) * LANES)
    return jnp.concatenate([high[:, lanes], high[:, lanes], low[:, lanes]], axis=1)


def pick_heads(value):
    cells = value.reshape(WLON, 2 * GROUP, LANES)
    lane = lax.broadcasted_iota(jnp.int32, (WLON, GROUP, LANES), 2)
    return jnp.where(lane < HEAD, cells[:, :GROUP], cells[:, GROUP:]).reshape(ROWS, LANES)


def main_kernel(
    comm,
    feat_hbm, cot_hbm, gain_hbm, shift_hbm, qkv_hbm, out_hbm, table_hbm, perm_hbm,
    *refs,
):
    if not comm:
        spare, refs = refs[4], refs[:4] + refs[5:]
    (
        grad_ref, piece, gathered, last,
        feat_ref, cot_ref, gain_ref, shift_ref, qkv_ref, out_ref, table_ref, perm_ref, load_sem,
        halo_out, halo_in, win, back_out, unit, cot, inv, hid,
        qh, ql, kh, kl, vh, vl, gh_, gl_,
        strip, turned, qst, gst, scores, dattn, ah, al, dh, dl, lanes,
        wsend, xsend, nsend, bsend, wcore, xcore, ncore, wsum, xsum, wrecv, xrecv, nsum, nrecv,
        brecv, ypart, yrecv, zsend, zrecv, ysend,
        send_p, recv_p, send_c, recv_c, send_h, recv_h, send_x, recv_x, send_n, recv_n, send_b, recv_b,
        send_y, recv_y, send_g, recv_g, send_z, recv_z, send_l, recv_l,
    ) = refs
    if comm:
        lat, lon = lax.axis_index("lat"), lax.axis_index("lon")
    else:
        lat, lon = jnp.int32(0), jnp.int32(0)
    count = NZ * NY
    z, y = lon // NY, lax.rem(lon, NY)
    k, core = lat // 2, lax.rem(lat, 2)
    right, left = {"lon": lax.rem(lon + 1, count)}, {"lon": lax.rem(lon + count - 1, count)}
    partner = {"lat": k * 2 + 1 - core}

    def at_k(i):
        return {"lat": lax.rem(k + i, NK) * 2 + core}

    def at_z(i):
        return {"lon": lax.rem(z + i, NZ) * NY + y}

    def at_y(i):
        return {"lon": z * NY + lax.rem(y + i, NY)}

    def remote(src, dst, send, recv, device):
        return pltpu.make_async_remote_copy(
            src_ref=src, dst_ref=dst, send_sem=send, recv_sem=recv, device_id=device, device_id_type=MESH
        )

    def start_all(copies):
        for copy in copies if comm else ():
            copy.start()

    def wait_all(copies):
        for copy in copies if comm else ():
            copy.wait()

    def exchange(n, mine, where, src, dst, send, recv):
        for i in FAR_FIRST[n] if comm else ():
            other = lax.rem(mine + i, n)
            remote(src(other), dst.at[mine], send.at[i], recv.at[mine], where(i)).start()

    def finish(n, mine, where, src, dst, send, recv):
        for i in FAR_FIRST[n][::-1] if comm else ():
            other = lax.rem(mine + i, n)
            copy = remote(src(other), dst.at[other], send.at[i], recv.at[other], where(i))
            copy.wait_recv()
            copy.wait_send()

    def total(ref, n):
        return functools.reduce(lambda a, b: a + b, [ref[s] for s in range(n)])

    if comm:
        barrier = pltpu.get_barrier_semaphore()
        everyone = [left, right]
        everyone += [at_y(i) for i in FAR_FIRST[NY]] + [at_z(i) for i in FAR_FIRST[NZ]]
        everyone += [at_k(i) for i in FAR_FIRST[NK]] + [partner]
        for device in everyone:
            pl.semaphore_signal(barrier, inc=1, device_id=device, device_id_type=MESH)

    loads = [
        pltpu.make_async_copy(src, dst, load_sem.at[i])
        for i, (src, dst) in enumerate(
            (
                (feat_hbm, feat_ref), (cot_hbm, cot_ref), (gain_hbm, gain_ref), (shift_hbm, shift_ref),
                (qkv_hbm, qkv_ref), (out_hbm, out_ref), (table_hbm, table_ref), (perm_hbm, perm_ref),
            )
        )
    ]
    for load in loads:
        load.start()

    def tiles(slabs, first):
        for x in range(HALF):
            for i, slab in enumerate(slabs):
                f = feat_ref[:, first + x, slab, :]
                c = cot_ref[:, first + x, slab, :]
                mixed = jnp.concatenate([f[:, 128:], c[:, 128:]], axis=1)
                yield x * 2 + i, (f[:, :128], mixed, c[:, :128])

    loads[0].wait()
    loads[1].wait()
    for d, (slabs, first) in enumerate((((3, 0), HALF), ((1, 2), 0))):
        for g, parts in tiles(slabs, first):
            for t in range(3):
                halo_out[d, t * PIECES + g] = parts[t]
    if comm:
        pl.semaphore_wait(barrier, 3 + NY - 1 + NZ - 1 + NK - 1)
    cuts = (pl.ds(0, 2 * PIECES), pl.ds(2 * PIECES, PIECES))
    halo = [
        [
            remote(halo_out.at[d, cut], halo_in.at[d, cut], send_p.at[2 * e + d], recv_p.at[2 * e + d], (right, left)[d])
            for d in range(2)
        ]
        for e, cut in enumerate(cuts)
    ]
    start_all(halo[0])
    start_all(halo[1])
    gap = jnp.zeros((2, 128), F32)
    for base, slabs, first in ((HROWS, (3, 0), 0), (2 * HROWS, (1, 2), HALF)):
        for g, parts in tiles(slabs, first):
            for t in range(3):
                win[t, pl.ds(base + g * 8, 8), :] = jnp.concatenate([parts[t], gap], axis=0)

    def arrived(which):
        for d, base in ((0, 0), (1, 3 * HROWS)):
            for t in which:
                for g in range(PIECES):
                    source = halo_in if comm else halo_out
                    win[t, pl.ds(base + g * 8, 8), :] = jnp.concatenate(
                        [source[d, t * PIECES + g], gap], axis=0
                    )

    for load in loads[2:6]:
        load.wait()
    gain = gain_ref[...]
    shift = shift_ref[...]
    wq, wk, wv = (qkv_ref[:, e * D : (e + 1) * D] for e in range(3))
    wo = out_ref[...]
    scale = HEAD ** (-0.5)

    def keep(at, value, high, low):
        high[at, :], low[at, :] = split(value, 2)

    def project_features(first, rows):
        at = pl.ds(first, rows)
        f = jnp.concatenate([win[0, at, :], win[1, at, :][:, :64]], axis=1)
        centred = f - jnp.sum(f, axis=1, keepdims=True) * (1.0 / D)
        inverse = lax.rsqrt(jnp.sum(centred * centred, axis=1, keepdims=True) * (1.0 / D) + EPSILON)
        standard = centred * inverse
        hidden = standard * gain + shift
        unit[at, :] = standard
        inv[at, :] = inverse
        hid[at, :] = hidden
        keep(at, nn(hidden, wq) * scale, qh, ql)
        keep(at, nn(hidden, wk), kh, kl)
        keep(at, nn(hidden, wv), vh, vl)

    def project_cotangent(first, rows):
        at = pl.ds(first, rows)
        c = jnp.concatenate([win[2, at, :], win[1, at, :][:, 64:]], axis=1)
        cot[at, :] = c
        keep(at, nt(c, wo), gh_, gl_)

    project_features(HROWS, 2 * HROWS)
    project_cotangent(HROWS, 2 * HROWS)
    loads[6].wait()
    loads[7].wait()
    bias_strips(table_ref, perm_ref, turned, strip)

    wait_all(halo[0])
    arrived((0, 1))
    project_features(0, HROWS)
    project_features(3 * HROWS, HROWS)
    windows = [pl.ds(w * ROWS, ROWS) for w in range(PW)]
    for w, own in enumerate(windows):
        for p in range(PAIRS_OF_HEADS):
            rows = pair_rows(qh[own, :], ql[own, :], p)
            qst[w, p] = rows
            part = nt(rows, pair_cols(kh[own, :], kl[own, :], p), None)
            scores[w, :, p * 32 : p * 32 + 32, :] = part.reshape(WLON, 32, ROWS)

    wait_all(halo[1])
    arrived((2,))
    project_cotangent(0, HROWS)
    project_cotangent(3 * HROWS, HROWS)
    for w, own in enumerate(windows):
        for p in range(PAIRS_OF_HEADS):
            rows = pair_rows(gh_[own, :], gl_[own, :], p)
            gst[w, p] = rows
            part = nt(rows, pair_cols(vh[own, :], vl[own, :], p), None)
            dattn[w, :, p * 32 : p * 32 + 32, :] = part.reshape(WLON, 32, ROWS)

    nothing = jnp.zeros((BLOCK, 128), F32)
    for w in range(PW):
        turns = [None] * 8
        for x in range(WLON):
            s = scores[w, x] + strip[w, x]
            e = jnp.exp(s - jnp.max(s, axis=1, keepdims=True))
            a = e * (1.0 / jnp.sum(e, axis=1, keepdims=True))
            da = dattn[w, x]
            ds = a * (da - jnp.sum(a * da, axis=1, keepdims=True))
            ah[w, x], al[w, x] = split(a, 2)
            dh[w, x], dl[w, x] = split(ds, 2)
            turn, tile = (WLON - 1 - x) % 8, (WLON - 1 - x) // 8
            two = jnp.concatenate([ds, jnp.zeros((BLOCK, 256 - ROWS), F32)], axis=1)
            wide = jnp.concatenate([nothing, two] if tile else [two, nothing], axis=1)
            turns[turn] = wide if turns[turn] is None else turns[turn] + wide
        dband = turns[0]
        for turn in range(1, 8):
            dband = dband + pltpu.roll(turns[turn], turn * GROUP, 1)
        turned[:, :BLOCK] = dband.T
        for n in range(POS):
            row = (n // WLAT) * 8 + n % WLAT
            lanes[pl.ds(w * 24, 24), n * 128 : n * 128 + 128] = turned[pl.ds(row, 24, stride=GROUP), :]

    perm = perm_ref[...]
    sums = sum(nn(part, perm, None) for part in split(lanes[...], 2))
    for t in range(7):
        bsend[t] = sums[:, t * 128 : (t + 1) * 128]
    bsend[7] = jnp.zeros((48, 128), F32)
    step_b = (NZ, z, at_z, lambda o: bsend.at[o], brecv, send_b, recv_b)
    exchange(*step_b)

    def pair_of(ref, w, p):
        return ref[w, :, p * 32 : p * 32 + 32, :].reshape(PSTACK, ROWS)

    def applied(high, low, other_high, other_low):
        result = []
        for w, own in enumerate(windows):
            cols = []
            for p in range(PAIRS_OF_HEADS):
                at = slice(p * LANES, (p + 1) * LANES)
                oh = other_high[own, :][:, at]
                both = nn(pair_of(high, w, p), jnp.concatenate([oh, other_low[own, :][:, at]], axis=1), None)
                rest = nn(pair_of(low, w, p), oh, None)
                cols.append(pick_heads(both[:, :LANES] + both[:, LANES:] + rest))
            result.append(jnp.concatenate(cols, axis=1))
        return jnp.concatenate(result, axis=0)

    def gathered_keys(high, low, stack):
        result = []
        for w in range(PW):
            cols = []
            for p in range(PAIRS_OF_HEADS):
                rows = stack[w, p]
                both = tn(pair_of(high, w, p), rows[:, : 2 * LANES], None)
                rest = tn(pair_of(low, w, p), rows[:, :LANES], None)
                cols.append(both[:, :LANES] + both[:, LANES:] + rest)
            result.append(jnp.concatenate(cols, axis=1))
        return jnp.concatenate(result, axis=0)

    def cut(ref, one, two):
        columns = [
            one[:, :128], two[:, :128],
            jnp.concatenate([one[:, 128:], two[:, 128:]], axis=1),
        ]
        for l in range(LAT):
            for g in range(3):
                ref[l % 2, l // 2, pl.ds(g * 12, 12), :] = columns[g][l * 12 : (l + 1) * 12]

    mixture = applied(ah, al, vh, vl)
    dv = gathered_keys(ah, al, gst)
    hidden = hid[...]
    cut(wsend, tn(hidden, dv), tn(mixture, cot[...]))
    swap = [
        remote(wsend.at[1 - core], wcore, send_c.at[0], recv_c.at[0], partner),
        remote(xsend.at[1 - core], xcore, send_c.at[1], recv_c.at[1], partner),
        remote(nsend, ncore, send_c.at[2], recv_c.at[2], partner),
    ]
    start_all(swap[:1])

    dq = applied(dh, dl, kh, kl) * scale
    step_h = (NK, k, at_k, lambda o: wsum.at[o], wrecv, send_h, recv_h)
    step_x = (NK, k, at_k, lambda o: xsum.at[o], xrecv, send_x, recv_x)
    wait_all(swap[:1])
    if comm:
        for o in range(NK):
            wsum[o] = wsend[core, o] + wcore[o]
        exchange(*step_h)
        wrecv[k] = wsum[k]

    dk = gathered_keys(dh, dl, qst)
    cut(xsend, tn(hidden, dq), tn(hidden, dk))
    start_all(swap[1:2])

    gh = nt(dq, wq) + nt(dk, wk) + nt(dv, wv)
    standard = unit[...]
    ggain = jnp.sum(gh * standard, axis=0, keepdims=True)
    gshift = jnp.sum(gh, axis=0, keepdims=True)
    nsend[...] = jnp.concatenate(
        [
            ggain[:, :128], gshift[:, :128],
            jnp.concatenate([ggain[:, 128:], gshift[:, 128:]], axis=1),
            jnp.zeros((1, 128), F32),
        ],
        axis=0,
    )
    start_all(swap[2:])
    wait_all(swap[1:2])
    if comm:
        for o in range(NK):
            xsum[o] = xsend[core, o] + xcore[o]
        exchange(*step_x)
        xrecv[k] = xsum[k]

    gu = gh * gain
    mean_gu = jnp.sum(gu, axis=1, keepdims=True) * (1.0 / D)
    mean_uu = jnp.sum(gu * standard, axis=1, keepdims=True) * (1.0 / D)
    grad_ref[...] = cot[...] + inv[...] * (gu - mean_gu - standard * mean_uu)
    for d, base in ((0, 0), (1, 3 * HROWS)):
        for g in range(PIECES):
            back_out[d, g] = grad_ref[pl.ds(base + g * 8, WLAT), :]
    backs = [
        remote(back_out.at[d], piece.at[d], send_p.at[4 + d], recv_p.at[4 + d], (left, right)[d])
        for d in range(2)
    ]
    start_all(backs)
    if not comm:
        gathered[...] = bsend[...]
        spare[0] = wsend[...]
        spare[1] = xsend[...]
        last[0, 0:4, :] = nsend[...]
        return

    wait_all(swap[2:])
    step_n = (NK, k, at_k, lambda o: nsum, nrecv, send_n, recv_n)
    nsum[...] = nsend[...] + ncore[...]
    exchange(*step_n)
    nrecv[k] = nsum[...]

    step_y = (NY, y, at_y, lambda o: ypart, yrecv, send_y, recv_y)
    step_g = (NZ, z, at_z, lambda o: gathered.at[z], gathered, send_g, recv_g)
    step_z = (NZ, z, at_z, lambda o: zsend.at[o], zrecv, send_z, recv_z)
    step_l = (NY, y, at_y, lambda o: ysend, last, send_l, recv_l)

    brecv[z] = bsend[z]
    finish(*step_b)
    ypart[...] = total(brecv, NZ)
    exchange(*step_y)
    yrecv[y] = ypart[...]

    finish(*step_h)
    block_vo = total(wrecv, NK)
    finish(*step_x)
    block_qk = total(xrecv, NK)
    finish(*step_n)
    norm = total(nrecv, NK)[0:3]
    lane = lax.broadcasted_iota(jnp.int32, (12, 128), 1)
    for t in range(NZ):
        block = block_qk if t < 4 else block_vo
        e = (t // 2) % 2
        main = block[e * 12 : e * 12 + 12]
        if t % 2:
            tail = pltpu.roll(block[24:36], 96 if e else 32, 1)
            main = jnp.where(lane < 32, pltpu.roll(main, 32, 1), tail)
        zsend[t, 0:12, :] = main
        zsend[t, 12:15, :] = norm
        zsend[t, 15:16, :] = jnp.zeros((1, 128), F32)
    exchange(*step_z)
    zrecv[z] = zsend[z]

    finish(*step_y)
    gathered[z] = total(yrecv, NY)
    exchange(*step_g)

    finish(*step_z)
    ysend[...] = total(zrecv, NZ)
    exchange(*step_l)
    last[y] = ysend[...]

    wait_all(backs)
    finish(*step_g)
    finish(*step_l)


def main_call(comm, operands):
    vmem = pl.BlockSpec(memory_space=pltpu.VMEM)
    hbm = pl.BlockSpec(memory_space=pltpu.HBM)
    dma = pltpu.SemaphoreType.DMA
    sems = []
    for n in (6, 3, NK, NK, NK, NZ, NY, NZ, NZ, NY):
        sems += [dma((n,)), dma((n,))]

    def buf(*shape):
        return pltpu.VMEM(shape, F32)

    def half(*shape):
        return pltpu.VMEM(shape, BF16)

    full = buf(PW * ROWS, D)
    token = half(PW * ROWS, D)
    stack = half(PW, PAIRS_OF_HEADS, PSTACK, 3 * LANES)
    square = (PW, WLON, BLOCK, ROWS)
    outs = (
        jax.ShapeDtypeStruct((PW * ROWS, D), F32),
        jax.ShapeDtypeStruct((PW, PIECES, WLAT, D), F32),
        jax.ShapeDtypeStruct((NZ, 48, 128), F32),
        jax.ShapeDtypeStruct((NY, 16, 128), F32),
    )
    params = dict(vmem_limit_bytes=VLIM)
    if comm:
        params.update(collective_id=0, has_side_effects=True)
    else:
        outs += (jax.ShapeDtypeStruct((2, 2, NK, 36, 128), F32),)
    return pl.pallas_call(
        functools.partial(main_kernel, comm),
        out_shape=outs,
        in_specs=[hbm] * 8,
        out_specs=(vmem,) * len(outs),
        scratch_shapes=[pltpu.VMEM(t.shape, t.dtype) for t in operands] + [
            dma((8,)),
            buf(2, 3 * PIECES, WLAT, 128), buf(2, 3 * PIECES, WLAT, 128), buf(3, PW * ROWS, 128),
            buf(2, PIECES, WLAT, D),
            full, full, buf(PW * ROWS, 1), full,
            token, token, token, token, token, token, token, token,
            buf(*square), buf(STRIP, 128), stack, stack, buf(*square), buf(*square),
            half(*square), half(*square), half(*square), half(*square), buf(48, POS * 128),
            buf(2, NK, 36, 128), buf(2, NK, 36, 128), buf(4, 128), buf(NZ, 48, 128),
            buf(NK, 36, 128), buf(NK, 36, 128), buf(4, 128),
            buf(NK, 36, 128), buf(NK, 36, 128), buf(NK, 36, 128), buf(NK, 36, 128), buf(4, 128), buf(NK, 4, 128),
            buf(NZ, 48, 128), buf(48, 128), buf(NY, 48, 128),
            buf(NZ, 16, 128), buf(NZ, 16, 128), buf(16, 128),
        ] + sems,
        compiler_params=pltpu.CompilerParams(**params),
        name="window_block",
    )(*(pltpu.with_memory_space_constraint(t, pltpu.HBM) for t in operands))


def unpack_kernel(grad_ref, piece, gathered, last, feat_ref, weight_ref, bias_ref, norm_ref):
    y = lax.rem(lax.axis_index("lon"), NY)
    for x in range(HALF):
        for c, slabs in ((0, (3, 0)), (1, (1, 2))):
            for i, slab in enumerate(slabs):
                row = x * GROUP + i * 8
                own = grad_ref[pl.ds((1 + c) * HROWS + row, 8), :]
                own, far = own[:WLAT], piece[c, x * 2 + i]
                west, east = (own, far) if c == 0 else (far, own)
                feat_ref[:, x, slab, :] = west
                feat_ref[:, HALF + x, slab, :] = east
    for h in range(HEADS):
        main = gathered[h]
        rem = gathered[6]
        rem = rem if h == 0 else pltpu.roll(rem, 128 - 16 * h, 1)
        for c in range(PW):
            bias_ref[h, :, c, 0:128] = main[c * 24 : c * 24 + LONREL]
            bias_ref[h, :, c, 128:144] = rem[c * 24 : c * 24 + LONREL, :16]
    both = functools.reduce(lambda a, b: a + b, [last[s] for s in range(NY)]) * (1.0 / 384.0)
    rows = both[0:12]
    mine = rows[:, 0:24]
    for t in range(1, NY):
        mine = jnp.where(y == t, pltpu.roll(rows, 128 - 24 * t, 1)[:, 0:24], mine)
    weight_ref[...] = mine
    norm_ref[0:1, 0:128] = both[12:13]
    norm_ref[1:2, 0:128] = both[13:14]
    norm_ref[0:1, 128:192] = both[14:15, 0:64]
    norm_ref[1:2, 128:192] = both[14:15, 64:128]


def unpack(operands):
    vmem = pl.BlockSpec(memory_space=pltpu.VMEM)
    return pl.pallas_call(
        unpack_kernel,
        out_shape=(
            jax.ShapeDtypeStruct((WLAT, WLON, 4, D), F32),
            jax.ShapeDtypeStruct((12, 24), F32),
            jax.ShapeDtypeStruct((HEADS, LONREL, PW, PAIRS), F32),
            jax.ShapeDtypeStruct((2, D), F32),
        ),
        in_specs=[vmem] * 4,
        out_specs=(vmem,) * 4,
        compiler_params=pltpu.CompilerParams(vmem_limit_bytes=8 * 1024 * 1024),
        name="unpack",
    )(*operands)


def operands_of(features, cotangent, norm_gain, norm_shift, qkv_weight, out_weight, bias_table):
    return (
        features.transpose(1, 2, 0, 3),
        cotangent.transpose(1, 2, 0, 3),
        norm_gain.reshape(1, D),
        norm_shift.reshape(1, D),
        qkv_weight,
        out_weight,
        bias_table.reshape(PW, HEADS, LONREL, PAIRS).transpose(1, 2, 0, 3),
        jnp.asarray(permutation(), jnp.bfloat16),
    )


def shards(*args):
    grad_features, grad_weights, grad_bias, grad_norm = unpack(main_call(True, operands_of(*args)))
    return (
        grad_features.transpose(2, 0, 1, 3),
        grad_weights,
        grad_bias.transpose(2, 0, 1, 3).reshape(1, PW, HEADS, LONREL, PAIRS),
        grad_norm,
    )


def solution(mesh):
    placed = (
        P(None, "lat", "lon", None),
        P(None, "lat", "lon", None),
        P(),
        P(),
        P(),
        P(),
        P("lat", None, None, None, None),
    )
    return jax.shard_map(
        shards,
        mesh=mesh,
        in_specs=placed,
        out_specs=(
            P(None, "lat", "lon", None),
            P("lat", "lon"),
            P("lat", None, None, None, None),
            P(),
        ),
        check_vma=False,
    )
```

```python
import functools

import jax
import jax.numpy as jnp
import numpy as np
from jax import lax
from jax.experimental import pallas as pl
from jax.experimental.pallas import tpu as pltpu
from jax.sharding import PartitionSpec as P

D = 192
HEADS = 6
HEAD = 32
WLAT = 6
WLON = 12
HALF = WLON // 2
PW = 2
LONREL = 23
PAIRS = 144
EPSILON = 1e-05

GROUP = 16
ROWS = WLON * GROUP
HROWS = HALF * GROUP
PSTACK = 2 * ROWS
PIECES = 2 * HALF
BF16 = jnp.bfloat16
BLOCK = HEADS * GROUP
STRIP = 24 * GROUP
POS = 12
TABW = 896
NEG = -1e30
PAIRS_OF_HEADS = 3
LANES = 2 * HEAD
F32 = jnp.float32
HIGH = lax.Precision.HIGH
MESH = pl.DeviceIdType.MESH
LAT = 16
NK = 8
NZ = 8
NY = 4
FAR_FIRST = {4: (2, 1, 3), 8: (4, 3, 5, 2, 6, 1, 7)}
NLON = NZ * NY
AROUND = sorted(
    ((dz, dy) for dz in range(NZ) for dy in range(NY) if dz or dy),
    key=lambda t: -(min(t[0], NZ - t[0]) + 2 * min(t[1], NY - t[1])),
)
VLIM = 32 * 1024 * 1024


def permutation():
    out = np.zeros((POS * 128, TABW), np.float32)
    for n in range(POS):
        j, b = divmod(n, WLAT)
        for h in range(HEADS):
            for i in range(2):
                for a in range(WLAT):
                    p = ((i * 2 + j) * WLAT + a) * WLAT + b
                    col = h * 128 + p if p < 128 else 768 + h * 16 + p - 128
                    out[n * 128 + h * GROUP + i * 8 + a, col] = 1.0
    return out


def nn(a, b, precision=HIGH):
    return lax.dot_general(a, b, (((1,), (0,)), ((), ())), precision=precision, preferred_element_type=F32)


def nt(a, b, precision=HIGH):
    return lax.dot_general(a, b, (((1,), (1,)), ((), ())), precision=precision, preferred_element_type=F32)


def tn(a, b, precision=HIGH):
    return lax.dot_general(a, b, (((0,), (0,)), ((), ())), precision=precision, preferred_element_type=F32)


def split(x, terms):
    parts = []
    for _ in range(terms):
        part = x.astype(jnp.bfloat16)
        parts.append(part)
        x = x - part.astype(F32)
    return parts


def strip_mask(c):
    lane = lax.broadcasted_iota(jnp.int32, (BLOCK, STRIP), 1)
    row = lax.broadcasted_iota(jnp.int32, (BLOCK, STRIP), 0)
    shut = (lane & 7) >= WLAT
    if c == 0:
        shut = shut | (((lane >> 3) & 1) != ((row >> 3) & 1))
    return jnp.where(shut, NEG, 0.0)


def bias_strips(table_ref, perm_ref, turned, strip):
    zero_row = jnp.zeros((1, 128), F32)
    rem_row = jnp.zeros((1, 16), F32)
    mains, rems = [], []
    for c in range(PW):
        main, rem = [], []
        for h in range(HEADS):
            t = table_ref[h, :, c, :]
            main.append(jnp.concatenate([t[:, :128], zero_row], axis=0))
            rem.append(jnp.concatenate([t[:, 128:], rem_row], axis=0))
        rem.append(jnp.zeros((24, 32), F32))
        mains.append(jnp.concatenate(main, axis=1))
        rems.append(jnp.concatenate(rem, axis=1))
    table = jnp.concatenate(
        [jnp.concatenate(mains, axis=0), jnp.concatenate(rems, axis=0)], axis=1
    )
    perm = perm_ref[...]
    spread = sum(nt(part, perm, None) for part in split(table, 3))
    for c in range(PW):
        for n in range(POS):
            row = (n // WLAT) * 8 + n % WLAT
            turned[pl.ds(row, 24, stride=GROUP), :] = spread[c * 24 : c * 24 + 24, n * 128 : n * 128 + 128]
        for n in (6, 7, 14, 15):
            turned[pl.ds(n, 24, stride=GROUP), :] = jnp.zeros((24, 128), F32)
        band = turned[...].T[:BLOCK, :] + strip_mask(c)
        for x in range(WLON):
            move = (WLON - 1 - x) * GROUP
            strip[c, x] = (band if move == 0 else pltpu.roll(band, STRIP - move, 1))[:, :ROWS]


def parity_lanes(width):
    lane = lax.broadcasted_iota(jnp.int32, (1, width), 1)
    second = ((lane >> 5) & 1).astype(F32)
    return (1.0 - second).astype(BF16), second.astype(BF16)


def pair_rows(high, low, p):
    lanes = slice(p * LANES, (p + 1) * LANES)
    joined = jnp.concatenate([high[:, lanes], low[:, lanes], high[:, lanes]], axis=1)
    first, second = parity_lanes(3 * LANES)
    cells = joined.reshape(WLON, GROUP, 3 * LANES)
    return jnp.concatenate([cells * first, cells * second], axis=1).reshape(PSTACK, 3 * LANES)


def pair_cols(high, low, p):
    lanes = slice(p * LANES, (p + 1) * LANES)
    return jnp.concatenate([high[:, lanes], high[:, lanes], low[:, lanes]], axis=1)


def pick_heads(value):
    cells = value.reshape(WLON, 2 * GROUP, LANES)
    lane = lax.broadcasted_iota(jnp.int32, (WLON, GROUP, LANES), 2)
    return jnp.where(lane < HEAD, cells[:, :GROUP], cells[:, GROUP:]).reshape(ROWS, LANES)


def main_kernel(
    comm,
    feat_hbm, cot_hbm, gain_hbm, shift_hbm, qkv_hbm, out_hbm, table_hbm, perm_hbm,
    *refs,
):
    if not comm:
        spare, refs = refs[4], refs[:4] + refs[5:]
    (
        grad_ref, piece, gathered, last,
        feat_ref, cot_ref, gain_ref, shift_ref, qkv_ref, out_ref, table_ref, perm_ref, load_sem,
        halo_out, halo_in, win, back_out, unit, cot, inv, hid,
        qh, ql, kh, kl, vh, vl, gh_, gl_,
        strip, turned, qst, gst, scores, dattn, ah, al, dh, dl, lanes,
        wsend, xsend, nsend, bsend, wcore, xcore, ncore, wsum, xsum, wrecv, xrecv, nsum, nrecv,
        brecv, zsend, zrecv,
        send_p, recv_p, send_c, recv_c, send_h, recv_h, send_x, recv_x, send_n, recv_n, send_b, recv_b,
        send_g, recv_g, send_l, recv_l,
    ) = refs
    if comm:
        lat, lon = lax.axis_index("lat"), lax.axis_index("lon")
    else:
        lat, lon = jnp.int32(0), jnp.int32(0)
    count = NZ * NY
    z, y = lon // NY, lax.rem(lon, NY)
    k, core = lat // 2, lax.rem(lat, 2)
    right, left = {"lon": lax.rem(lon + 1, count)}, {"lon": lax.rem(lon + count - 1, count)}
    partner = {"lat": k * 2 + 1 - core}

    def at_k(i):
        return {"lat": lax.rem(k + i, NK) * 2 + core}

    def lon_of(dz, dy):
        return lax.rem(z + dz, NZ) * NY + lax.rem(y + dy, NY)

    def remote(src, dst, send, recv, device):
        return pltpu.make_async_remote_copy(
            src_ref=src, dst_ref=dst, send_sem=send, recv_sem=recv, device_id=device, device_id_type=MESH
        )

    def start_all(copies):
        for copy in copies if comm else ():
            copy.start()

    def wait_all(copies):
        for copy in copies if comm else ():
            copy.wait()

    lon_peers = [(lon_of(dz, dy), {"lon": lon_of(dz, dy)}) for dz, dy in AROUND]
    k_peers = [(lax.rem(k + i, NK), at_k(i)) for i in FAR_FIRST[NK]]

    def exchange(peers, mine, src, dst, send, recv):
        for i, (other, device) in enumerate(peers if comm else ()):
            remote(src(other), dst.at[mine], send.at[i], recv.at[mine], device).start()

    def finish(peers, mine, src, dst, send, recv):
        for i, (other, device) in list(enumerate(peers if comm else ()))[::-1]:
            copy = remote(src(other), dst.at[other], send.at[i], recv.at[other], device)
            copy.wait_recv()
            copy.wait_send()

    def total(ref, n):
        return functools.reduce(lambda a, b: a + b, [ref[s] for s in range(n)])

    if comm:
        barrier = pltpu.get_barrier_semaphore()
        everyone = [left, right]
        everyone += [{"lon": lax.rem(lon + i, count)} for i in range(2, count - 1)]
        everyone += [device for _, device in k_peers] + [partner]
        for device in everyone:
            pl.semaphore_signal(barrier, inc=1, device_id=device, device_id_type=MESH)

    loads = [
        pltpu.make_async_copy(src, dst, load_sem.at[i])
        for i, (src, dst) in enumerate(
            (
                (feat_hbm, feat_ref), (cot_hbm, cot_ref), (gain_hbm, gain_ref), (shift_hbm, shift_ref),
                (qkv_hbm, qkv_ref), (out_hbm, out_ref), (table_hbm, table_ref), (perm_hbm, perm_ref),
            )
        )
    ]
    for load in loads:
        load.start()

    def tiles(slabs, first):
        for x in range(HALF):
            for i, slab in enumerate(slabs):
                f = feat_ref[:, first + x, slab, :]
                c = cot_ref[:, first + x, slab, :]
                mixed = jnp.concatenate([f[:, 128:], c[:, 128:]], axis=1)
                yield x * 2 + i, (f[:, :128], mixed, c[:, :128])

    loads[0].wait()
    loads[1].wait()
    for d, (slabs, first) in enumerate((((3, 0), HALF), ((1, 2), 0))):
        for g, parts in tiles(slabs, first):
            for t in range(3):
                halo_out[d, t * PIECES + g] = parts[t]
    if comm:
        pl.semaphore_wait(barrier, len(everyone))
    cuts = (pl.ds(0, 2 * PIECES), pl.ds(2 * PIECES, PIECES))
    halo = [
        [
            remote(halo_out.at[d, cut], halo_in.at[d, cut], send_p.at[2 * e + d], recv_p.at[2 * e + d], (right, left)[d])
            for d in range(2)
        ]
        for e, cut in enumerate(cuts)
    ]
    start_all(halo[0])
    start_all(halo[1])
    gap = jnp.zeros((2, 128), F32)
    for base, slabs, first in ((HROWS, (3, 0), 0), (2 * HROWS, (1, 2), HALF)):
        for g, parts in tiles(slabs, first):
            for t in range(3):
                win[t, pl.ds(base + g * 8, 8), :] = jnp.concatenate([parts[t], gap], axis=0)

    def arrived(which):
        for d, base in ((0, 0), (1, 3 * HROWS)):
            for t in which:
                for g in range(PIECES):
                    source = halo_in if comm else halo_out
                    win[t, pl.ds(base + g * 8, 8), :] = jnp.concatenate(
                        [source[d, t * PIECES + g], gap], axis=0
                    )

    for load in loads[2:6]:
        load.wait()
    gain = gain_ref[...]
    shift = shift_ref[...]
    wq, wk, wv = (qkv_ref[:, e * D : (e + 1) * D] for e in range(3))
    wo = out_ref[...]
    scale = HEAD ** (-0.5)

    def keep(at, value, high, low):
        high[at, :], low[at, :] = split(value, 2)

    def project_features(first, rows):
        at = pl.ds(first, rows)
        f = jnp.concatenate([win[0, at, :], win[1, at, :][:, :64]], axis=1)
        centred = f - jnp.sum(f, axis=1, keepdims=True) * (1.0 / D)
        inverse = lax.rsqrt(jnp.sum(centred * centred, axis=1, keepdims=True) * (1.0 / D) + EPSILON)
        standard = centred * inverse
        hidden = standard * gain + shift
        unit[at, :] = standard
        inv[at, :] = inverse
        hid[at, :] = hidden
        keep(at, nn(hidden, wq) * scale, qh, ql)
        keep(at, nn(hidden, wk), kh, kl)
        keep(at, nn(hidden, wv), vh, vl)

    def project_cotangent(first, rows):
        at = pl.ds(first, rows)
        c = jnp.concatenate([win[2, at, :], win[1, at, :][:, 64:]], axis=1)
        cot[at, :] = c
        keep(at, nt(c, wo), gh_, gl_)

    project_features(HROWS, 2 * HROWS)
    project_cotangent(HROWS, 2 * HROWS)
    loads[6].wait()
    loads[7].wait()
    bias_strips(table_ref, perm_ref, turned, strip)

    wait_all(halo[0])
    arrived((0, 1))
    project_features(0, HROWS)
    project_features(3 * HROWS, HROWS)
    windows = [pl.ds(w * ROWS, ROWS) for w in range(PW)]
    for w, own in enumerate(windows):
        for p in range(PAIRS_OF_HEADS):
            rows = pair_rows(qh[own, :], ql[own, :], p)
            qst[w, p] = rows
            part = nt(rows, pair_cols(kh[own, :], kl[own, :], p), None)
            scores[w, :, p * 32 : p * 32 + 32, :] = part.reshape(WLON, 32, ROWS)

    wait_all(halo[1])
    arrived((2,))
    project_cotangent(0, HROWS)
    project_cotangent(3 * HROWS, HROWS)
    for w, own in enumerate(windows):
        for p in range(PAIRS_OF_HEADS):
            rows = pair_rows(gh_[own, :], gl_[own, :], p)
            gst[w, p] = rows
            part = nt(rows, pair_cols(vh[own, :], vl[own, :], p), None)
            dattn[w, :, p * 32 : p * 32 + 32, :] = part.reshape(WLON, 32, ROWS)

    nothing = jnp.zeros((BLOCK, 128), F32)
    for w in range(PW):
        turns = [None] * 8
        for x in range(WLON):
            s = scores[w, x] + strip[w, x]
            e = jnp.exp(s - jnp.max(s, axis=1, keepdims=True))
            a = e * (1.0 / jnp.sum(e, axis=1, keepdims=True))
            da = dattn[w, x]
            ds = a * (da - jnp.sum(a * da, axis=1, keepdims=True))
            ah[w, x], al[w, x] = split(a, 2)
            dh[w, x], dl[w, x] = split(ds, 2)
            turn, tile = (WLON - 1 - x) % 8, (WLON - 1 - x) // 8
            two = jnp.concatenate([ds, jnp.zeros((BLOCK, 256 - ROWS), F32)], axis=1)
            wide = jnp.concatenate([nothing, two] if tile else [two, nothing], axis=1)
            turns[turn] = wide if turns[turn] is None else turns[turn] + wide
        dband = turns[0]
        for turn in range(1, 8):
            dband = dband + pltpu.roll(turns[turn], turn * GROUP, 1)
        turned[:, :BLOCK] = dband.T
        for n in range(POS):
            row = (n // WLAT) * 8 + n % WLAT
            lanes[pl.ds(w * 24, 24), n * 128 : n * 128 + 128] = turned[pl.ds(row, 24, stride=GROUP), :]

    perm = perm_ref[...]
    sums = sum(nn(part, perm, None) for part in split(lanes[...], 2))
    for t in range(7):
        for q in range(NY):
            bsend[t * NY + q] = sums[q * 12 : (q + 1) * 12, t * 128 : (t + 1) * 128]
    bsend[pl.ds(28, 4)] = jnp.zeros((4, 12, 128), F32)
    step_b = (lon_peers, lon, lambda o: bsend.at[o], brecv, send_b, recv_b)
    exchange(*step_b)

    def pair_of(ref, w, p):
        return ref[w, :, p * 32 : p * 32 + 32, :].reshape(PSTACK, ROWS)

    def applied(high, low, other_high, other_low):
        result = []
        for w, own in enumerate(windows):
            cols = []
            for p in range(PAIRS_OF_HEADS):
                at = slice(p * LANES, (p + 1) * LANES)
                oh = other_high[own, :][:, at]
                both = nn(pair_of(high, w, p), jnp.concatenate([oh, other_low[own, :][:, at]], axis=1), None)
                rest = nn(pair_of(low, w, p), oh, None)
                cols.append(pick_heads(both[:, :LANES] + both[:, LANES:] + rest))
            result.append(jnp.concatenate(cols, axis=1))
        return jnp.concatenate(result, axis=0)

    def gathered_keys(high, low, stack):
        result = []
        for w in range(PW):
            cols = []
            for p in range(PAIRS_OF_HEADS):
                rows = stack[w, p]
                both = tn(pair_of(high, w, p), rows[:, : 2 * LANES], None)
                rest = tn(pair_of(low, w, p), rows[:, :LANES], None)
                cols.append(both[:, :LANES] + both[:, LANES:] + rest)
            result.append(jnp.concatenate(cols, axis=1))
        return jnp.concatenate(result, axis=0)

    def cut(ref, one, two):
        columns = [
            one[:, :128], two[:, :128],
            jnp.concatenate([one[:, 128:], two[:, 128:]], axis=1),
        ]
        for l in range(LAT):
            for g in range(3):
                ref[l % 2, l // 2, pl.ds(g * 12, 12), :] = columns[g][l * 12 : (l + 1) * 12]

    mixture = applied(ah, al, vh, vl)
    dv = gathered_keys(ah, al, gst)
    hidden = hid[...]
    cut(wsend, tn(hidden, dv), tn(mixture, cot[...]))
    swap = [
        remote(wsend.at[1 - core], wcore, send_c.at[0], recv_c.at[0], partner),
        remote(xsend.at[1 - core], xcore, send_c.at[1], recv_c.at[1], partner),
        remote(nsend, ncore, send_c.at[2], recv_c.at[2], partner),
    ]
    start_all(swap[:1])

    dq = applied(dh, dl, kh, kl) * scale
    step_h = (k_peers, k, lambda o: wsum.at[o], wrecv, send_h, recv_h)
    step_x = (k_peers, k, lambda o: xsum.at[o], xrecv, send_x, recv_x)
    wait_all(swap[:1])
    if comm:
        for o in range(NK):
            wsum[o] = wsend[core, o] + wcore[o]
        exchange(*step_h)
        wrecv[k] = wsum[k]

    dk = gathered_keys(dh, dl, qst)
    cut(xsend, tn(hidden, dq), tn(hidden, dk))
    start_all(swap[1:2])

    gh = nt(dq, wq) + nt(dk, wk) + nt(dv, wv)
    standard = unit[...]
    ggain = jnp.sum(gh * standard, axis=0, keepdims=True)
    gshift = jnp.sum(gh, axis=0, keepdims=True)
    lead = jnp.zeros((4, 32), F32)
    fours = [t[:, u : u + 96] for t in (ggain, gshift) for u in (0, 96)]
    nsend[...] = jnp.concatenate([lead, jnp.concatenate(fours, axis=0)], axis=1)
    start_all(swap[2:])
    wait_all(swap[1:2])
    if comm:
        for o in range(NK):
            xsum[o] = xsend[core, o] + xcore[o]
        exchange(*step_x)
        xrecv[k] = xsum[k]

    gu = gh * gain
    mean_gu = jnp.sum(gu, axis=1, keepdims=True) * (1.0 / D)
    mean_uu = jnp.sum(gu * standard, axis=1, keepdims=True) * (1.0 / D)
    grad_ref[...] = cot[...] + inv[...] * (gu - mean_gu - standard * mean_uu)
    for d, base in ((0, 0), (1, 3 * HROWS)):
        for g in range(PIECES):
            back_out[d, g] = grad_ref[pl.ds(base + g * 8, WLAT), :]
    backs = [
        remote(back_out.at[d], piece.at[d], send_p.at[4 + d], recv_p.at[4 + d], (left, right)[d])
        for d in range(2)
    ]
    start_all(backs)
    if not comm:
        gathered[...] = bsend[...]
        spare[0] = wsend[...]
        spare[1] = xsend[...]
        last[0:4, :] = nsend[...]
        return

    wait_all(swap[2:])
    step_n = (k_peers, k, lambda o: nsum, nrecv, send_n, recv_n)
    nsum[...] = nsend[...] + ncore[...]
    exchange(*step_n)
    nrecv[k] = nsum[...]

    step_g = (lon_peers, lon, lambda o: gathered.at[lon], gathered, send_g, recv_g)
    step_l = (lon_peers, lon, lambda o: zsend.at[o], zrecv, send_l, recv_l)

    brecv[lon] = bsend[lon]
    finish(*step_b)
    gathered[lon] = total(brecv, NLON)
    exchange(*step_g)

    finish(*step_h)
    block_vo = total(wrecv, NK)
    finish(*step_n)
    norm = jnp.concatenate([total(nrecv, NK), jnp.zeros((4, 128), F32)], axis=0)
    finish(*step_x)
    block_qk = total(xrecv, NK)
    lane = lax.broadcasted_iota(jnp.int32, (12, 128), 1)
    lane8 = lax.broadcasted_iota(jnp.int32, (8, 128), 1)
    row8 = lax.broadcasted_iota(jnp.int32, (8, 128), 0)
    for t in range(NZ):
        block = block_qk if t < 4 else block_vo
        e = (t // 2) % 2
        main = block[e * 12 : e * 12 + 12]
        if t % 2:
            tail = pltpu.roll(block[24:36], 96 if e else 32, 1)
            main = jnp.where(lane < 32, pltpu.roll(main, 32, 1), tail)
        top, low = main[0:8], main[4:12]
        for q in range(NY):
            above = top if q == 0 else pltpu.roll(top, 128 - 24 * q, 1)
            below = pltpu.roll(low, (160 - 24 * q) % 128, 1)
            zsend[t * NY + q] = jnp.where(lane8 < 24, above, jnp.where(row8 < 4, norm, below))
    exchange(*step_l)
    zrecv[lon] = zsend[lon]

    wait_all(backs)
    finish(*step_g)
    finish(*step_l)
    last[...] = total(zrecv, NLON)


def main_call(comm, operands):
    vmem = pl.BlockSpec(memory_space=pltpu.VMEM)
    hbm = pl.BlockSpec(memory_space=pltpu.HBM)
    dma = pltpu.SemaphoreType.DMA
    sems = []
    for n in (6, 3, NK, NK, NK, NLON, NLON, NLON):
        sems += [dma((n,)), dma((n,))]

    def buf(*shape):
        return pltpu.VMEM(shape, F32)

    def half(*shape):
        return pltpu.VMEM(shape, BF16)

    full = buf(PW * ROWS, D)
    token = half(PW * ROWS, D)
    stack = half(PW, PAIRS_OF_HEADS, PSTACK, 3 * LANES)
    square = (PW, WLON, BLOCK, ROWS)
    outs = (
        jax.ShapeDtypeStruct((PW * ROWS, D), F32),
        jax.ShapeDtypeStruct((PW, PIECES, WLAT, D), F32),
        jax.ShapeDtypeStruct((NLON, 12, 128), F32),
        jax.ShapeDtypeStruct((8, 128), F32),
    )
    params = dict(vmem_limit_bytes=VLIM)
    if comm:
        params.update(collective_id=0, has_side_effects=True)
    else:
        outs += (jax.ShapeDtypeStruct((2, 2, NK, 36, 128), F32),)
    return pl.pallas_call(
        functools.partial(main_kernel, comm),
        out_shape=outs,
        in_specs=[hbm] * 8,
        out_specs=(vmem,) * len(outs),
        scratch_shapes=[pltpu.VMEM(t.shape, t.dtype) for t in operands] + [
            dma((8,)),
            buf(2, 3 * PIECES, WLAT, 128), buf(2, 3 * PIECES, WLAT, 128), buf(3, PW * ROWS, 128),
            buf(2, PIECES, WLAT, D),
            full, full, buf(PW * ROWS, 1), full,
            token, token, token, token, token, token, token, token,
            buf(*square), buf(STRIP, 128), stack, stack, buf(*square), buf(*square),
            half(*square), half(*square), half(*square), half(*square), buf(48, POS * 128),
            buf(2, NK, 36, 128), buf(2, NK, 36, 128), buf(4, 128), buf(NLON, 12, 128),
            buf(NK, 36, 128), buf(NK, 36, 128), buf(4, 128),
            buf(NK, 36, 128), buf(NK, 36, 128), buf(NK, 36, 128), buf(NK, 36, 128), buf(4, 128), buf(NK, 4, 128),
            buf(NLON, 12, 128), buf(NLON, 8, 128), buf(NLON, 8, 128),
        ] + sems,
        compiler_params=pltpu.CompilerParams(**params),
        name="window_block",
    )(*(pltpu.with_memory_space_constraint(t, pltpu.HBM) for t in operands))


def unpack_kernel(grad_ref, piece, gathered, last, feat_ref, weight_ref, bias_ref, norm_ref):
    for x in range(HALF):
        for c, slabs in ((0, (3, 0)), (1, (1, 2))):
            for i, slab in enumerate(slabs):
                row = x * GROUP + i * 8
                own = grad_ref[pl.ds((1 + c) * HROWS + row, 8), :]
                own, far = own[:WLAT], piece[c, x * 2 + i]
                west, east = (own, far) if c == 0 else (far, own)
                feat_ref[:, x, slab, :] = west
                feat_ref[:, HALF + x, slab, :] = east
    for h in range(HEADS):
        for q in range(NY):
            rows = 12 if q % 2 == 0 else LONREL - 12
            at = pl.ds(12 * (q % 2), rows)
            rem = gathered[24 + q]
            rem = rem if h == 0 else pltpu.roll(rem, 128 - 16 * h, 1)
            bias_ref[h, at, q // 2, 0:128] = gathered[h * NY + q][:rows]
            bias_ref[h, at, q // 2, 128:144] = rem[:rows, :16]
    both = last[...] * (1.0 / 384.0)
    weight_ref[0:8, :] = both[:, 0:24]
    weight_ref[8:12, :] = both[4:8, 32:56]
    for e in range(2):
        norm_ref[e : e + 1, 0:96] = both[2 * e : 2 * e + 1, 32:128]
        norm_ref[e : e + 1, 96:192] = both[2 * e + 1 : 2 * e + 2, 32:128]


def unpack(operands):
    vmem = pl.BlockSpec(memory_space=pltpu.VMEM)
    return pl.pallas_call(
        unpack_kernel,
        out_shape=(
            jax.ShapeDtypeStruct((WLAT, WLON, 4, D), F32),
            jax.ShapeDtypeStruct((12, 24), F32),
            jax.ShapeDtypeStruct((HEADS, LONREL, PW, PAIRS), F32),
            jax.ShapeDtypeStruct((2, D), F32),
        ),
        in_specs=[vmem] * 4,
        out_specs=(vmem,) * 4,
        compiler_params=pltpu.CompilerParams(vmem_limit_bytes=8 * 1024 * 1024),
        name="unpack",
    )(*operands)


def operands_of(features, cotangent, norm_gain, norm_shift, qkv_weight, out_weight, bias_table):
    return (
        features.transpose(1, 2, 0, 3),
        cotangent.transpose(1, 2, 0, 3),
        norm_gain.reshape(1, D),
        norm_shift.reshape(1, D),
        qkv_weight,
        out_weight,
        bias_table.reshape(PW, HEADS, LONREL, PAIRS).transpose(1, 2, 0, 3),
        jnp.asarray(permutation(), jnp.bfloat16),
    )


def shards(*args):
    grad_features, grad_weights, grad_bias, grad_norm = unpack(main_call(True, operands_of(*args)))
    return (
        grad_features.transpose(2, 0, 1, 3),
        grad_weights,
        grad_bias.transpose(2, 0, 1, 3).reshape(1, PW, HEADS, LONREL, PAIRS),
        grad_norm,
    )


def solution(mesh):
    placed = (
        P(None, "lat", "lon", None),
        P(None, "lat", "lon", None),
        P(),
        P(),
        P(),
        P(),
        P("lat", None, None, None, None),
    )
    return jax.shard_map(
        shards,
        mesh=mesh,
        in_specs=placed,
        out_specs=(
            P(None, "lat", "lon", None),
            P("lat", "lon"),
            P("lat", None, None, None, None),
            P(),
        ),
        check_vma=False,
    )
```

```python
import functools

import jax
import jax.numpy as jnp
import numpy as np
from jax import lax
from jax.experimental import pallas as pl
from jax.experimental.pallas import tpu as pltpu
from jax.sharding import PartitionSpec as P

D = 192
HEADS = 6
HEAD = 32
WLAT = 6
WLON = 12
HALF = WLON // 2
PW = 2
LONREL = 23
PAIRS = 144
EPSILON = 1e-05

GROUP = 16
ROWS = WLON * GROUP
HROWS = HALF * GROUP
PSTACK = 2 * ROWS
PIECES = 2 * HALF
BF16 = jnp.bfloat16
BLOCK = HEADS * GROUP
STRIP = 24 * GROUP
POS = 12
TABW = 896
NEG = -1e30
PAIRS_OF_HEADS = 3
LANES = 2 * HEAD
F32 = jnp.float32
HIGH = lax.Precision.HIGH
MESH = pl.DeviceIdType.MESH
LAT = 16
NK = 8
NZ = 8
NY = 4
FAR_FIRST = {4: (2, 1, 3), 8: (4, 3, 5, 2, 6, 1, 7)}
NLON = NZ * NY
AROUND = sorted(
    ((dz, dy) for dz in range(NZ) for dy in range(NY) if dz or dy),
    key=lambda t: -(min(t[0], NZ - t[0]) + 2 * min(t[1], NY - t[1])),
)
VLIM = 32 * 1024 * 1024


def permutation():
    out = np.zeros((POS * 128, TABW), np.float32)
    for n in range(POS):
        j, b = divmod(n, WLAT)
        for h in range(HEADS):
            for i in range(2):
                for a in range(WLAT):
                    p = ((i * 2 + j) * WLAT + a) * WLAT + b
                    col = h * 128 + p if p < 128 else 768 + h * 16 + p - 128
                    out[n * 128 + h * GROUP + i * 8 + a, col] = 1.0
    return out


def nn(a, b, precision=HIGH):
    return lax.dot_general(a, b, (((1,), (0,)), ((), ())), precision=precision, preferred_element_type=F32)


def nt(a, b, precision=HIGH):
    return lax.dot_general(a, b, (((1,), (1,)), ((), ())), precision=precision, preferred_element_type=F32)


def tn(a, b, precision=HIGH):
    return lax.dot_general(a, b, (((0,), (0,)), ((), ())), precision=precision, preferred_element_type=F32)


def split(x, terms):
    parts = []
    for _ in range(terms):
        part = x.astype(jnp.bfloat16)
        parts.append(part)
        x = x - part.astype(F32)
    return parts


def strip_mask(c):
    lane = lax.broadcasted_iota(jnp.int32, (BLOCK, STRIP), 1)
    row = lax.broadcasted_iota(jnp.int32, (BLOCK, STRIP), 0)
    shut = (lane & 7) >= WLAT
    if c == 0:
        shut = shut | (((lane >> 3) & 1) != ((row >> 3) & 1))
    return jnp.where(shut, NEG, 0.0)


def bias_strips(table_ref, perm_ref, turned, strip):
    zero_row = jnp.zeros((1, 128), F32)
    rem_row = jnp.zeros((1, 16), F32)
    mains, rems = [], []
    for c in range(PW):
        main, rem = [], []
        for h in range(HEADS):
            t = table_ref[h, :, c, :]
            main.append(jnp.concatenate([t[:, :128], zero_row], axis=0))
            rem.append(jnp.concatenate([t[:, 128:], rem_row], axis=0))
        rem.append(jnp.zeros((24, 32), F32))
        mains.append(jnp.concatenate(main, axis=1))
        rems.append(jnp.concatenate(rem, axis=1))
    table = jnp.concatenate(
        [jnp.concatenate(mains, axis=0), jnp.concatenate(rems, axis=0)], axis=1
    )
    perm = perm_ref[...]
    spread = sum(nt(part, perm, None) for part in split(table, 3))
    for c in range(PW):
        for n in range(POS):
            row = (n // WLAT) * 8 + n % WLAT
            turned[pl.ds(row, 24, stride=GROUP), :] = spread[c * 24 : c * 24 + 24, n * 128 : n * 128 + 128]
        for n in (6, 7, 14, 15):
            turned[pl.ds(n, 24, stride=GROUP), :] = jnp.zeros((24, 128), F32)
        band = turned[...].T[:BLOCK, :] + strip_mask(c)
        for x in range(WLON):
            move = (WLON - 1 - x) * GROUP
            strip[c, x] = (band if move == 0 else pltpu.roll(band, STRIP - move, 1))[:, :ROWS]


def parity_lanes(width):
    lane = lax.broadcasted_iota(jnp.int32, (1, width), 1)
    second = ((lane >> 5) & 1).astype(F32)
    return (1.0 - second).astype(BF16), second.astype(BF16)


def pair_rows(high, low, p):
    lanes = slice(p * LANES, (p + 1) * LANES)
    joined = jnp.concatenate([high[:, lanes], low[:, lanes], high[:, lanes]], axis=1)
    first, second = parity_lanes(3 * LANES)
    cells = joined.reshape(WLON, GROUP, 3 * LANES)
    return jnp.concatenate([cells * first, cells * second], axis=1).reshape(PSTACK, 3 * LANES)


def pair_cols(high, low, p):
    lanes = slice(p * LANES, (p + 1) * LANES)
    return jnp.concatenate([high[:, lanes], high[:, lanes], low[:, lanes]], axis=1)


def pick_heads(value):
    cells = value.reshape(WLON, 2 * GROUP, LANES)
    lane = lax.broadcasted_iota(jnp.int32, (WLON, GROUP, LANES), 2)
    return jnp.where(lane < HEAD, cells[:, :GROUP], cells[:, GROUP:]).reshape(ROWS, LANES)


def main_kernel(
    comm,
    feat_hbm, cot_hbm, gain_hbm, shift_hbm, qkv_hbm, out_hbm, table_hbm, perm_hbm,
    *refs,
):
    if not comm:
        spare, refs = refs[4], refs[:4] + refs[5:]
    (
        grad_ref, piece, gathered, last,
        feat_ref, cot_ref, gain_ref, shift_ref, qkv_ref, out_ref, table_ref, perm_ref, load_sem,
        halo_out, halo_in, win, back_out, unit, cot, inv, hid,
        qh, ql, kh, kl, vh, vl, gh_, gl_,
        strip, turned, qst, gst, scores, dattn, ah, al, dh, dl, lanes,
        wsend, xsend, nsend, bsend, wcore, xcore, ncore, wsum, xsum, wrecv, xrecv, nsum, nrecv,
        brecv, zsend, zrecv,
        send_p, recv_p, send_c, recv_c, send_h, recv_h, send_x, recv_x, send_n, recv_n, send_b, recv_b,
        send_g, recv_g, send_s, recv_s, send_l, recv_l,
    ) = refs
    if comm:
        lat, lon = lax.axis_index("lat"), lax.axis_index("lon")
    else:
        lat, lon = jnp.int32(0), jnp.int32(0)
    count = NZ * NY
    z, y = lon // NY, lax.rem(lon, NY)
    k, core = lat // 2, lax.rem(lat, 2)
    right, left = {"lon": lax.rem(lon + 1, count)}, {"lon": lax.rem(lon + count - 1, count)}
    partner = {"lat": k * 2 + 1 - core}

    def at_k(i):
        return {"lat": lax.rem(k + i, NK) * 2 + core}

    def lon_of(dz, dy):
        return lax.rem(z + dz, NZ) * NY + lax.rem(y + dy, NY)

    def remote(src, dst, send, recv, device):
        return pltpu.make_async_remote_copy(
            src_ref=src, dst_ref=dst, send_sem=send, recv_sem=recv, device_id=device, device_id_type=MESH
        )

    def start_all(copies):
        for copy in copies if comm else ():
            copy.start()

    def wait_all(copies):
        for copy in copies if comm else ():
            copy.wait()

    lon_peers = [(lon_of(dz, dy), {"lon": lon_of(dz, dy)}) for dz, dy in AROUND]
    k_peers = [(lax.rem(k + i, NK), at_k(i)) for i in FAR_FIRST[NK]]

    def exchange(peers, mine, src, dst, send, recv):
        for i, (other, device) in enumerate(peers if comm else ()):
            remote(src(other), dst.at[mine], send.at[i], recv.at[mine], device).start()

    def finish(peers, mine, src, dst, send, recv):
        for i, (other, device) in list(enumerate(peers if comm else ()))[::-1]:
            copy = remote(src(other), dst.at[other], send.at[i], recv.at[other], device)
            copy.wait_recv()
            copy.wait_send()

    def total(ref, n):
        return functools.reduce(lambda a, b: a + b, [ref[s] for s in range(n)])

    if comm:
        barrier = pltpu.get_barrier_semaphore()
        everyone = [left, right]
        everyone += [{"lon": lax.rem(lon + i, count)} for i in range(2, count - 1)]
        everyone += [device for _, device in k_peers] + [partner]
        for device in everyone:
            pl.semaphore_signal(barrier, inc=1, device_id=device, device_id_type=MESH)

    loads = [
        pltpu.make_async_copy(src, dst, load_sem.at[i])
        for i, (src, dst) in enumerate(
            (
                (feat_hbm, feat_ref), (cot_hbm, cot_ref), (gain_hbm, gain_ref), (shift_hbm, shift_ref),
                (qkv_hbm, qkv_ref), (out_hbm, out_ref), (table_hbm, table_ref), (perm_hbm, perm_ref),
            )
        )
    ]
    for load in loads:
        load.start()

    def tiles(slabs, first):
        for x in range(HALF):
            for i, slab in enumerate(slabs):
                f = feat_ref[:, first + x, slab, :]
                c = cot_ref[:, first + x, slab, :]
                mixed = jnp.concatenate([f[:, 128:], c[:, 128:]], axis=1)
                yield x * 2 + i, (f[:, :128], mixed, c[:, :128])

    loads[0].wait()
    loads[1].wait()
    for d, (slabs, first) in enumerate((((3, 0), HALF), ((1, 2), 0))):
        for g, parts in tiles(slabs, first):
            for t in range(3):
                halo_out[d, t * PIECES + g] = parts[t]
    if comm:
        pl.semaphore_wait(barrier, len(everyone))
    cuts = (pl.ds(0, 2 * PIECES), pl.ds(2 * PIECES, PIECES))
    halo = [
        [
            remote(halo_out.at[d, cut], halo_in.at[d, cut], send_p.at[2 * e + d], recv_p.at[2 * e + d], (right, left)[d])
            for d in range(2)
        ]
        for e, cut in enumerate(cuts)
    ]
    start_all(halo[0])
    start_all(halo[1])
    gap = jnp.zeros((2, 128), F32)
    for base, slabs, first in ((HROWS, (3, 0), 0), (2 * HROWS, (1, 2), HALF)):
        for g, parts in tiles(slabs, first):
            for t in range(3):
                win[t, pl.ds(base + g * 8, 8), :] = jnp.concatenate([parts[t], gap], axis=0)

    def arrived(which):
        for d, base in ((0, 0), (1, 3 * HROWS)):
            for t in which:
                for g in range(PIECES):
                    source = halo_in if comm else halo_out
                    win[t, pl.ds(base + g * 8, 8), :] = jnp.concatenate(
                        [source[d, t * PIECES + g], gap], axis=0
                    )

    for load in loads[2:6]:
        load.wait()
    gain = gain_ref[...]
    shift = shift_ref[...]
    wq, wk, wv = (qkv_ref[:, e * D : (e + 1) * D] for e in range(3))
    wo = out_ref[...]
    scale = HEAD ** (-0.5)

    def keep(at, value, high, low):
        high[at, :], low[at, :] = split(value, 2)

    def project_features(first, rows):
        at = pl.ds(first, rows)
        f = jnp.concatenate([win[0, at, :], win[1, at, :][:, :64]], axis=1)
        centred = f - jnp.sum(f, axis=1, keepdims=True) * (1.0 / D)
        inverse = lax.rsqrt(jnp.sum(centred * centred, axis=1, keepdims=True) * (1.0 / D) + EPSILON)
        standard = centred * inverse
        hidden = standard * gain + shift
        unit[at, :] = standard
        inv[at, :] = inverse
        hid[at, :] = hidden
        keep(at, nn(hidden, wq) * scale, qh, ql)
        keep(at, nn(hidden, wk), kh, kl)
        keep(at, nn(hidden, wv), vh, vl)

    def project_cotangent(first, rows):
        at = pl.ds(first, rows)
        c = jnp.concatenate([win[2, at, :], win[1, at, :][:, 64:]], axis=1)
        cot[at, :] = c
        keep(at, nt(c, wo), gh_, gl_)

    project_features(HROWS, 2 * HROWS)
    project_cotangent(HROWS, 2 * HROWS)
    loads[6].wait()
    loads[7].wait()
    bias_strips(table_ref, perm_ref, turned, strip)

    wait_all(halo[0])
    arrived((0, 1))
    project_features(0, HROWS)
    project_features(3 * HROWS, HROWS)
    windows = [pl.ds(w * ROWS, ROWS) for w in range(PW)]
    for w, own in enumerate(windows):
        for p in range(PAIRS_OF_HEADS):
            rows = pair_rows(qh[own, :], ql[own, :], p)
            qst[w, p] = rows
            part = nt(rows, pair_cols(kh[own, :], kl[own, :], p), None)
            scores[w, :, p * 32 : p * 32 + 32, :] = part.reshape(WLON, 32, ROWS)

    wait_all(halo[1])
    arrived((2,))
    project_cotangent(0, HROWS)
    project_cotangent(3 * HROWS, HROWS)
    for w, own in enumerate(windows):
        for p in range(PAIRS_OF_HEADS):
            rows = pair_rows(gh_[own, :], gl_[own, :], p)
            gst[w, p] = rows
            part = nt(rows, pair_cols(vh[own, :], vl[own, :], p), None)
            dattn[w, :, p * 32 : p * 32 + 32, :] = part.reshape(WLON, 32, ROWS)

    nothing = jnp.zeros((BLOCK, 128), F32)
    for w in range(PW):
        turns = [None] * 8
        for x in range(WLON):
            s = scores[w, x] + strip[w, x]
            e = jnp.exp(s - jnp.max(s, axis=1, keepdims=True))
            a = e * (1.0 / jnp.sum(e, axis=1, keepdims=True))
            da = dattn[w, x]
            ds = a * (da - jnp.sum(a * da, axis=1, keepdims=True))
            ah[w, x], al[w, x] = split(a, 2)
            dh[w, x], dl[w, x] = split(ds, 2)
            turn, tile = (WLON - 1 - x) % 8, (WLON - 1 - x) // 8
            two = jnp.concatenate([ds, jnp.zeros((BLOCK, 256 - ROWS), F32)], axis=1)
            wide = jnp.concatenate([nothing, two] if tile else [two, nothing], axis=1)
            turns[turn] = wide if turns[turn] is None else turns[turn] + wide
        dband = turns[0]
        for turn in range(1, 8):
            dband = dband + pltpu.roll(turns[turn], turn * GROUP, 1)
        turned[:, :BLOCK] = dband.T
        for n in range(POS):
            row = (n // WLAT) * 8 + n % WLAT
            lanes[pl.ds(w * 24, 24), n * 128 : n * 128 + 128] = turned[pl.ds(row, 24, stride=GROUP), :]

    perm = perm_ref[...]
    sums = sum(nn(part, perm, None) for part in split(lanes[...], 2))
    for t in range(7):
        for q in range(NY):
            bsend[t * NY + q] = sums[q * 12 : (q + 1) * 12, t * 128 : (t + 1) * 128]
    bsend[pl.ds(28, 4)] = jnp.zeros((4, 12, 128), F32)
    step_b = (lon_peers, lon, lambda o: bsend.at[o], brecv, send_b, recv_b)
    exchange(*step_b)

    def pair_of(ref, w, p):
        return ref[w, :, p * 32 : p * 32 + 32, :].reshape(PSTACK, ROWS)

    def applied(high, low, other_high, other_low):
        result = []
        for w, own in enumerate(windows):
            cols = []
            for p in range(PAIRS_OF_HEADS):
                at = slice(p * LANES, (p + 1) * LANES)
                oh = other_high[own, :][:, at]
                both = nn(pair_of(high, w, p), jnp.concatenate([oh, other_low[own, :][:, at]], axis=1), None)
                rest = nn(pair_of(low, w, p), oh, None)
                cols.append(pick_heads(both[:, :LANES] + both[:, LANES:] + rest))
            result.append(jnp.concatenate(cols, axis=1))
        return jnp.concatenate(result, axis=0)

    def gathered_keys(high, low, stack):
        result = []
        for w in range(PW):
            cols = []
            for p in range(PAIRS_OF_HEADS):
                rows = stack[w, p]
                both = tn(pair_of(high, w, p), rows[:, : 2 * LANES], None)
                rest = tn(pair_of(low, w, p), rows[:, :LANES], None)
                cols.append(both[:, :LANES] + both[:, LANES:] + rest)
            result.append(jnp.concatenate(cols, axis=1))
        return jnp.concatenate(result, axis=0)

    def cut(ref, one, two):
        columns = [
            one[:, :128], two[:, :128],
            jnp.concatenate([one[:, 128:], two[:, 128:]], axis=1),
        ]
        for l in range(LAT):
            for g in range(3):
                ref[l % 2, l // 2, pl.ds(g * 12, 12), :] = columns[g][l * 12 : (l + 1) * 12]

    mixture = applied(ah, al, vh, vl)
    dv = gathered_keys(ah, al, gst)
    hidden = hid[...]
    cut(wsend, tn(hidden, dv), tn(mixture, cot[...]))
    swap = [
        remote(wsend.at[1 - core], wcore, send_c.at[0], recv_c.at[0], partner),
        remote(xsend.at[1 - core], xcore, send_c.at[1], recv_c.at[1], partner),
        remote(nsend, ncore, send_c.at[2], recv_c.at[2], partner),
    ]
    start_all(swap[:1])

    dq = applied(dh, dl, kh, kl) * scale
    step_h = (k_peers, k, lambda o: wsum.at[o], wrecv, send_h, recv_h)
    step_x = (k_peers, k, lambda o: xsum.at[o], xrecv, send_x, recv_x)
    wait_all(swap[:1])
    if comm:
        for o in range(NK):
            wsum[o] = wsend[core, o] + wcore[o]
        exchange(*step_h)
        wrecv[k] = wsum[k]

    dk = gathered_keys(dh, dl, qst)
    cut(xsend, tn(hidden, dq), tn(hidden, dk))
    start_all(swap[1:2])

    gh = nt(dq, wq) + nt(dk, wk) + nt(dv, wv)
    standard = unit[...]
    ggain = jnp.sum(gh * standard, axis=0, keepdims=True)
    gshift = jnp.sum(gh, axis=0, keepdims=True)
    lead = jnp.zeros((4, 32), F32)
    fours = [t[:, u : u + 96] for t in (ggain, gshift) for u in (0, 96)]
    nsend[...] = jnp.concatenate([lead, jnp.concatenate(fours, axis=0)], axis=1)
    start_all(swap[2:])
    wait_all(swap[1:2])
    if comm:
        for o in range(NK):
            xsum[o] = xsend[core, o] + xcore[o]
        exchange(*step_x)
        xrecv[k] = xsum[k]

    mine_z = pl.ds(z * NY, NY)
    y_peers = [(lon_of(0, i), {"lon": lon_of(0, i)}) for i in FAR_FIRST[NY]]
    step_g = (y_peers, lon, lambda o: gathered.at[lon], gathered, send_g, recv_g)
    if comm:
        brecv[lon] = bsend[lon]
        finish(*step_b)
        gathered[lon] = total(brecv, NLON)
        exchange(*step_g)

    gu = gh * gain
    mean_gu = jnp.sum(gu, axis=1, keepdims=True) * (1.0 / D)
    mean_uu = jnp.sum(gu * standard, axis=1, keepdims=True) * (1.0 / D)
    grad_ref[...] = cot[...] + inv[...] * (gu - mean_gu - standard * mean_uu)
    for d, base in ((0, 0), (1, 3 * HROWS)):
        cells = [grad_ref[pl.ds(base + g * 8, WLAT), :] for g in range(PIECES)]
        for g in range(PIECES):
            back_out[d, g] = cells[g][:, :128]
        for g in range(HALF):
            back_out[d, PIECES + g] = jnp.concatenate([cells[g][:, 128:], cells[HALF + g][:, 128:]], axis=1)
    backs = [
        remote(back_out.at[d], piece.at[d], send_p.at[4 + d], recv_p.at[4 + d], (left, right)[d])
        for d in range(2)
    ]
    start_all(backs)
    if not comm:
        gathered[...] = bsend[...]
        spare[0] = wsend[...]
        spare[1] = xsend[...]
        last[0:4, :] = nsend[...]
        return

    wait_all(swap[2:])
    step_n = (k_peers, k, lambda o: nsum, nrecv, send_n, recv_n)
    nsum[...] = nsend[...] + ncore[...]
    exchange(*step_n)
    nrecv[k] = nsum[...]

    step_l = (lon_peers, lon, lambda o: zsend.at[o], zrecv, send_l, recv_l)

    finish(*step_g)
    spread_z = [
        (remote(gathered.at[mine_z], gathered.at[mine_z], send_s.at[i], recv_s.at[z], {"lon": lon_of(dz, 0)}), dz)
        for i, dz in enumerate(FAR_FIRST[NZ])
    ]
    for copy, _ in spread_z:
        copy.start()

    finish(*step_h)
    block_vo = total(wrecv, NK)
    finish(*step_n)
    norm = jnp.concatenate([total(nrecv, NK), jnp.zeros((4, 128), F32)], axis=0)
    finish(*step_x)
    block_qk = total(xrecv, NK)
    lane = lax.broadcasted_iota(jnp.int32, (12, 128), 1)
    lane8 = lax.broadcasted_iota(jnp.int32, (8, 128), 1)
    row8 = lax.broadcasted_iota(jnp.int32, (8, 128), 0)
    for t in range(NZ):
        block = block_qk if t < 4 else block_vo
        e = (t // 2) % 2
        main = block[e * 12 : e * 12 + 12]
        if t % 2:
            tail = pltpu.roll(block[24:36], 96 if e else 32, 1)
            main = jnp.where(lane < 32, pltpu.roll(main, 32, 1), tail)
        top, low = main[0:8], main[4:12]
        for q in range(NY):
            above = top if q == 0 else pltpu.roll(top, 128 - 24 * q, 1)
            below = pltpu.roll(low, (160 - 24 * q) % 128, 1)
            zsend[t * NY + q] = jnp.where(lane8 < 24, above, jnp.where(row8 < 4, norm, below))
    exchange(*step_l)
    zrecv[lon] = zsend[lon]

    wait_all(backs)
    for i, (copy, dz) in list(enumerate(spread_z))[::-1]:
        other = lax.rem(z + dz, NZ)
        theirs = pl.ds(other * NY, NY)
        remote(gathered.at[theirs], gathered.at[theirs], send_s.at[i], recv_s.at[other], {"lon": lon_of(dz, 0)}).wait_recv()
        copy.wait_send()
    finish(*step_l)
    last[...] = total(zrecv, NLON)


def main_call(comm, operands):
    vmem = pl.BlockSpec(memory_space=pltpu.VMEM)
    hbm = pl.BlockSpec(memory_space=pltpu.HBM)
    dma = pltpu.SemaphoreType.DMA
    sems = []
    for n in (6, 3, NK, NK, NK, NLON, NLON, NZ, NLON):
        sems += [dma((n,)), dma((n,))]

    def buf(*shape):
        return pltpu.VMEM(shape, F32)

    def half(*shape):
        return pltpu.VMEM(shape, BF16)

    full = buf(PW * ROWS, D)
    token = half(PW * ROWS, D)
    stack = half(PW, PAIRS_OF_HEADS, PSTACK, 3 * LANES)
    square = (PW, WLON, BLOCK, ROWS)
    outs = (
        jax.ShapeDtypeStruct((PW * ROWS, D), F32),
        jax.ShapeDtypeStruct((PW, PIECES + HALF, WLAT, 128), F32),
        jax.ShapeDtypeStruct((NLON, 12, 128), F32),
        jax.ShapeDtypeStruct((8, 128), F32),
    )
    params = dict(vmem_limit_bytes=VLIM)
    if comm:
        params.update(collective_id=0, has_side_effects=True)
    else:
        outs += (jax.ShapeDtypeStruct((2, 2, NK, 36, 128), F32),)
    return pl.pallas_call(
        functools.partial(main_kernel, comm),
        out_shape=outs,
        in_specs=[hbm] * 8,
        out_specs=(vmem,) * len(outs),
        scratch_shapes=[pltpu.VMEM(t.shape, t.dtype) for t in operands] + [
            dma((8,)),
            buf(2, 3 * PIECES, WLAT, 128), buf(2, 3 * PIECES, WLAT, 128), buf(3, PW * ROWS, 128),
            buf(2, PIECES + HALF, WLAT, 128),
            full, full, buf(PW * ROWS, 1), full,
            token, token, token, token, token, token, token, token,
            buf(*square), buf(STRIP, 128), stack, stack, buf(*square), buf(*square),
            half(*square), half(*square), half(*square), half(*square), buf(48, POS * 128),
            buf(2, NK, 36, 128), buf(2, NK, 36, 128), buf(4, 128), buf(NLON, 12, 128),
            buf(NK, 36, 128), buf(NK, 36, 128), buf(4, 128),
            buf(NK, 36, 128), buf(NK, 36, 128), buf(NK, 36, 128), buf(NK, 36, 128), buf(4, 128), buf(NK, 4, 128),
            buf(NLON, 12, 128), buf(NLON, 8, 128), buf(NLON, 8, 128),
        ] + sems,
        compiler_params=pltpu.CompilerParams(**params),
        name="window_block",
    )(*(pltpu.with_memory_space_constraint(t, pltpu.HBM) for t in operands))


def unpack_kernel(grad_ref, piece, gathered, last, feat_ref, weight_ref, bias_ref, norm_ref):
    for x in range(HALF):
        for c, slabs in ((0, (3, 0)), (1, (1, 2))):
            for i, slab in enumerate(slabs):
                row = x * GROUP + i * 8
                own = grad_ref[pl.ds((1 + c) * HROWS + row, 8), :]
                g = x * 2 + i
                side = piece[c, PIECES + g % HALF]
                side = side[:, :64] if g < HALF else side[:, 64:]
                own, far = own[:WLAT], jnp.concatenate([piece[c, g], side], axis=1)
                west, east = (own, far) if c == 0 else (far, own)
                feat_ref[:, x, slab, :] = west
                feat_ref[:, HALF + x, slab, :] = east
    for h in range(HEADS):
        for q in range(NY):
            rows = 12 if q % 2 == 0 else LONREL - 12
            at = pl.ds(12 * (q % 2), rows)
            rem = gathered[24 + q]
            rem = rem if h == 0 else pltpu.roll(rem, 128 - 16 * h, 1)
            bias_ref[h, at, q // 2, 0:128] = gathered[h * NY + q][:rows]
            bias_ref[h, at, q // 2, 128:144] = rem[:rows, :16]
    both = last[...] * (1.0 / 384.0)
    weight_ref[0:8, :] = both[:, 0:24]
    weight_ref[8:12, :] = both[4:8, 32:56]
    for e in range(2):
        norm_ref[e : e + 1, 0:96] = both[2 * e : 2 * e + 1, 32:128]
        norm_ref[e : e + 1, 96:192] = both[2 * e + 1 : 2 * e + 2, 32:128]


def unpack(operands):
    vmem = pl.BlockSpec(memory_space=pltpu.VMEM)
    return pl.pallas_call(
        unpack_kernel,
        out_shape=(
            jax.ShapeDtypeStruct((WLAT, WLON, 4, D), F32),
            jax.ShapeDtypeStruct((12, 24), F32),
            jax.ShapeDtypeStruct((HEADS, LONREL, PW, PAIRS), F32),
            jax.ShapeDtypeStruct((2, D), F32),
        ),
        in_specs=[vmem] * 4,
        out_specs=(vmem,) * 4,
        compiler_params=pltpu.CompilerParams(vmem_limit_bytes=8 * 1024 * 1024),
        name="unpack",
    )(*operands)


def operands_of(features, cotangent, norm_gain, norm_shift, qkv_weight, out_weight, bias_table):
    return (
        features.transpose(1, 2, 0, 3),
        cotangent.transpose(1, 2, 0, 3),
        norm_gain.reshape(1, D),
        norm_shift.reshape(1, D),
        qkv_weight,
        out_weight,
        bias_table.reshape(PW, HEADS, LONREL, PAIRS).transpose(1, 2, 0, 3),
        jnp.asarray(permutation(), jnp.bfloat16),
    )


def shards(*args):
    grad_features, grad_weights, grad_bias, grad_norm = unpack(main_call(True, operands_of(*args)))
    return (
        grad_features.transpose(2, 0, 1, 3),
        grad_weights,
        grad_bias.transpose(2, 0, 1, 3).reshape(1, PW, HEADS, LONREL, PAIRS),
        grad_norm,
    )


def solution(mesh):
    placed = (
        P(None, "lat", "lon", None),
        P(None, "lat", "lon", None),
        P(),
        P(),
        P(),
        P(),
        P("lat", None, None, None, None),
    )
    return jax.shard_map(
        shards,
        mesh=mesh,
        in_specs=placed,
        out_specs=(
            P(None, "lat", "lon", None),
            P("lat", "lon"),
            P("lat", None, None, None, None),
            P(),
        ),
        check_vma=False,
    )
```

```python
import functools

import jax
import jax.numpy as jnp
import numpy as np
from jax import lax
from jax.experimental import pallas as pl
from jax.experimental.pallas import tpu as pltpu
from jax.sharding import PartitionSpec as P

D = 192
HEADS = 6
HEAD = 32
WLAT = 6
WLON = 12
HALF = WLON // 2
PW = 2
LONREL = 23
PAIRS = 144
EPSILON = 1e-05

GROUP = 16
ROWS = WLON * GROUP
HROWS = HALF * GROUP
PSTACK = 2 * ROWS
PIECES = 2 * HALF
BF16 = jnp.bfloat16
BLOCK = HEADS * GROUP
STRIP = 24 * GROUP
POS = 12
TABW = 896
NEG = -1e30
PAIRS_OF_HEADS = 3
LANES = 2 * HEAD
F32 = jnp.float32
HIGH = lax.Precision.HIGH
MESH = pl.DeviceIdType.MESH
LAT = 16
NK = 8
NZ = 8
NY = 4
FAR_FIRST = {4: (2, 1, 3), 8: (4, 3, 5, 2, 6, 1, 7)}
NLON = NZ * NY
AROUND = sorted(
    ((dz, dy) for dz in range(NZ) for dy in range(NY) if dz or dy),
    key=lambda t: -(min(t[0], NZ - t[0]) + 2 * min(t[1], NY - t[1])),
)
VLIM = 32 * 1024 * 1024


def permutation():
    out = np.zeros((POS * 128, TABW), np.float32)
    for n in range(POS):
        j, b = divmod(n, WLAT)
        for h in range(HEADS):
            for i in range(2):
                for a in range(WLAT):
                    p = ((i * 2 + j) * WLAT + a) * WLAT + b
                    col = h * 128 + p if p < 128 else 768 + h * 16 + p - 128
                    out[n * 128 + h * GROUP + i * 8 + a, col] = 1.0
    return out


def nn(a, b, precision=HIGH):
    return lax.dot_general(a, b, (((1,), (0,)), ((), ())), precision=precision, preferred_element_type=F32)


def nt(a, b, precision=HIGH):
    return lax.dot_general(a, b, (((1,), (1,)), ((), ())), precision=precision, preferred_element_type=F32)


def tn(a, b, precision=HIGH):
    return lax.dot_general(a, b, (((0,), (0,)), ((), ())), precision=precision, preferred_element_type=F32)


def split(x, terms):
    parts = []
    for _ in range(terms):
        part = x.astype(jnp.bfloat16)
        parts.append(part)
        x = x - part.astype(F32)
    return parts


def strip_mask(c):
    lane = lax.broadcasted_iota(jnp.int32, (BLOCK, STRIP), 1)
    row = lax.broadcasted_iota(jnp.int32, (BLOCK, STRIP), 0)
    shut = (lane & 7) >= WLAT
    if c == 0:
        shut = shut | (((lane >> 3) & 1) != ((row >> 3) & 1))
    return jnp.where(shut, NEG, 0.0)


def bias_strips(table_ref, perm_ref, turned, strip):
    zero_row = jnp.zeros((1, 128), F32)
    rem_row = jnp.zeros((1, 16), F32)
    mains, rems = [], []
    for c in range(PW):
        main, rem = [], []
        for h in range(HEADS):
            t = table_ref[h, :, c, :]
            main.append(jnp.concatenate([t[:, :128], zero_row], axis=0))
            rem.append(jnp.concatenate([t[:, 128:], rem_row], axis=0))
        rem.append(jnp.zeros((24, 32), F32))
        mains.append(jnp.concatenate(main, axis=1))
        rems.append(jnp.concatenate(rem, axis=1))
    table = jnp.concatenate(
        [jnp.concatenate(mains, axis=0), jnp.concatenate(rems, axis=0)], axis=1
    )
    perm = perm_ref[...]
    spread = sum(nt(part, perm, None) for part in split(table, 3))
    for c in range(PW):
        for n in range(POS):
            row = (n // WLAT) * 8 + n % WLAT
            turned[pl.ds(row, 24, stride=GROUP), :] = spread[c * 24 : c * 24 + 24, n * 128 : n * 128 + 128]
        for n in (6, 7, 14, 15):
            turned[pl.ds(n, 24, stride=GROUP), :] = jnp.zeros((24, 128), F32)
        band = turned[...].T[:BLOCK, :] + strip_mask(c)
        for x in range(WLON):
            move = (WLON - 1 - x) * GROUP
            strip[c, x] = (band if move == 0 else pltpu.roll(band, STRIP - move, 1))[:, :ROWS]


def parity_lanes(width):
    lane = lax.broadcasted_iota(jnp.int32, (1, width), 1)
    second = ((lane >> 5) & 1).astype(F32)
    return (1.0 - second).astype(BF16), second.astype(BF16)


def pair_rows(high, low, p):
    lanes = slice(p * LANES, (p + 1) * LANES)
    joined = jnp.concatenate([high[:, lanes], low[:, lanes], high[:, lanes]], axis=1)
    first, second = parity_lanes(3 * LANES)
    cells = joined.reshape(WLON, GROUP, 3 * LANES)
    return jnp.concatenate([cells * first, cells * second], axis=1).reshape(PSTACK, 3 * LANES)


def pair_cols(high, low, p):
    lanes = slice(p * LANES, (p + 1) * LANES)
    return jnp.concatenate([high[:, lanes], high[:, lanes], low[:, lanes]], axis=1)


def pick_heads(value):
    cells = value.reshape(WLON, 2 * GROUP, LANES)
    lane = lax.broadcasted_iota(jnp.int32, (WLON, GROUP, LANES), 2)
    return jnp.where(lane < HEAD, cells[:, :GROUP], cells[:, GROUP:]).reshape(ROWS, LANES)


def main_kernel(
    comm,
    feat_hbm, cot_hbm, gain_hbm, shift_hbm, qkv_hbm, out_hbm, table_hbm, perm_hbm,
    *refs,
):
    if not comm:
        spare, refs = refs[4], refs[:4] + refs[5:]
    (
        grad_ref, piece, gathered, last,
        feat_ref, cot_ref, gain_ref, shift_ref, qkv_ref, out_ref, table_ref, perm_ref, load_sem,
        halo_out, halo_in, win, back_out, unit, cot, inv, hid,
        qh, ql, kh, kl, vh, vl, gh_, gl_,
        strip, turned, qst, gst, scores, dattn, ah, al, dh, dl, lanes,
        wsend, xsend, nsend, bsend, wcore, xcore, ncore, wsum, xsum, wrecv, xrecv, nsum, nrecv,
        brecv, zsend, zrecv,
        send_p, recv_p, send_c, recv_c, send_h, recv_h, send_x, recv_x, send_n, recv_n, send_b, recv_b,
        send_g, recv_g, send_s, recv_s, send_l, recv_l,
    ) = refs
    if comm:
        lat, lon = lax.axis_index("lat"), lax.axis_index("lon")
    else:
        lat, lon = jnp.int32(0), jnp.int32(0)
    count = NZ * NY
    z, y = lon // NY, lax.rem(lon, NY)
    k, core = lat // 2, lax.rem(lat, 2)
    right, left = {"lon": lax.rem(lon + 1, count)}, {"lon": lax.rem(lon + count - 1, count)}
    partner = {"lat": k * 2 + 1 - core}

    def at_k(i):
        return {"lat": lax.rem(k + i, NK) * 2 + core}

    def lon_of(dz, dy):
        return lax.rem(z + dz, NZ) * NY + lax.rem(y + dy, NY)

    def remote(src, dst, send, recv, device):
        return pltpu.make_async_remote_copy(
            src_ref=src, dst_ref=dst, send_sem=send, recv_sem=recv, device_id=device, device_id_type=MESH
        )

    def start_all(copies):
        for copy in copies if comm else ():
            copy.start()

    def wait_all(copies):
        for copy in copies if comm else ():
            copy.wait()

    lon_peers = [(lon_of(dz, dy), {"lon": lon_of(dz, dy)}) for dz, dy in AROUND]
    k_peers = [(lax.rem(k + i, NK), at_k(i)) for i in FAR_FIRST[NK]]

    def exchange(peers, mine, src, dst, send, recv):
        for i, (other, device) in enumerate(peers if comm else ()):
            remote(src(other), dst.at[mine], send.at[i], recv.at[mine], device).start()

    def finish(peers, mine, src, dst, send, recv):
        for i, (other, device) in list(enumerate(peers if comm else ()))[::-1]:
            copy = remote(src(other), dst.at[other], send.at[i], recv.at[other], device)
            copy.wait_recv()
            copy.wait_send()

    def total(ref, n):
        return functools.reduce(lambda a, b: a + b, [ref[s] for s in range(n)])

    if comm:
        barrier = pltpu.get_barrier_semaphore()
        everyone = [left, right]
        everyone += [{"lon": lax.rem(lon + i, count)} for i in range(2, count - 1)]
        everyone += [device for _, device in k_peers] + [partner]
        for device in everyone:
            pl.semaphore_signal(barrier, inc=1, device_id=device, device_id_type=MESH)

    loads = [
        pltpu.make_async_copy(src, dst, load_sem.at[i])
        for i, (src, dst) in enumerate(
            (
                (feat_hbm, feat_ref), (cot_hbm, cot_ref), (gain_hbm, gain_ref), (shift_hbm, shift_ref),
                (qkv_hbm, qkv_ref), (out_hbm, out_ref), (table_hbm, table_ref), (perm_hbm, perm_ref),
            )
        )
    ]
    for load in loads:
        load.start()

    def tiles(slabs, first):
        for x in range(HALF):
            for i, slab in enumerate(slabs):
                f = feat_ref[:, first + x, slab, :]
                c = cot_ref[:, first + x, slab, :]
                mixed = jnp.concatenate([f[:, 128:], c[:, 128:]], axis=1)
                yield x * 2 + i, (f[:, :128], mixed, c[:, :128])

    loads[0].wait()
    loads[1].wait()
    for d, (slabs, first) in enumerate((((3, 0), HALF), ((1, 2), 0))):
        for g, parts in tiles(slabs, first):
            for t in range(3):
                halo_out[d, t * PIECES + g] = parts[t]
    if comm:
        pl.semaphore_wait(barrier, len(everyone))
    cuts = (pl.ds(0, 2 * PIECES), pl.ds(2 * PIECES, PIECES))
    halo = [
        [
            remote(halo_out.at[d, cut], halo_in.at[d, cut], send_p.at[2 * e + d], recv_p.at[2 * e + d], (right, left)[d])
            for d in range(2)
        ]
        for e, cut in enumerate(cuts)
    ]
    start_all(halo[0])
    start_all(halo[1])
    gap = jnp.zeros((2, 128), F32)
    for base, slabs, first in ((HROWS, (3, 0), 0), (2 * HROWS, (1, 2), HALF)):
        for g, parts in tiles(slabs, first):
            for t in range(3):
                win[t, pl.ds(base + g * 8, 8), :] = jnp.concatenate([parts[t], gap], axis=0)

    def arrived(which):
        for d, base in ((0, 0), (1, 3 * HROWS)):
            for t in which:
                for g in range(PIECES):
                    source = halo_in if comm else halo_out
                    win[t, pl.ds(base + g * 8, 8), :] = jnp.concatenate(
                        [source[d, t * PIECES + g], gap], axis=0
                    )

    for load in loads[2:6]:
        load.wait()
    gain = gain_ref[...]
    shift = shift_ref[...]
    wq, wk, wv = (qkv_ref[:, e * D : (e + 1) * D] for e in range(3))
    wo = out_ref[...]
    scale = HEAD ** (-0.5)

    def keep(at, value, high, low):
        high[at, :], low[at, :] = split(value, 2)

    def project_features(first, rows):
        at = pl.ds(first, rows)
        f = jnp.concatenate([win[0, at, :], win[1, at, :][:, :64]], axis=1)
        centred = f - jnp.sum(f, axis=1, keepdims=True) * (1.0 / D)
        inverse = lax.rsqrt(jnp.sum(centred * centred, axis=1, keepdims=True) * (1.0 / D) + EPSILON)
        standard = centred * inverse
        hidden = standard * gain + shift
        unit[at, :] = standard
        inv[at, :] = inverse
        hid[at, :] = hidden
        keep(at, nn(hidden, wq) * scale, qh, ql)
        keep(at, nn(hidden, wk), kh, kl)
        keep(at, nn(hidden, wv), vh, vl)

    def project_cotangent(first, rows):
        at = pl.ds(first, rows)
        c = jnp.concatenate([win[2, at, :], win[1, at, :][:, 64:]], axis=1)
        cot[at, :] = c
        keep(at, nt(c, wo), gh_, gl_)

    project_features(HROWS, 2 * HROWS)
    project_cotangent(HROWS, 2 * HROWS)
    loads[6].wait()
    loads[7].wait()
    bias_strips(table_ref, perm_ref, turned, strip)

    wait_all(halo[0])
    arrived((0, 1))
    project_features(0, HROWS)
    project_features(3 * HROWS, HROWS)
    windows = [pl.ds(w * ROWS, ROWS) for w in range(PW)]
    for w, own in enumerate(windows):
        for p in range(PAIRS_OF_HEADS):
            rows = pair_rows(qh[own, :], ql[own, :], p)
            qst[w, p] = rows
            part = nt(rows, pair_cols(kh[own, :], kl[own, :], p), None)
            scores[w, :, p * 32 : p * 32 + 32, :] = part.reshape(WLON, 32, ROWS)

    wait_all(halo[1])
    arrived((2,))
    project_cotangent(0, HROWS)
    project_cotangent(3 * HROWS, HROWS)
    for w, own in enumerate(windows):
        for p in range(PAIRS_OF_HEADS):
            rows = pair_rows(gh_[own, :], gl_[own, :], p)
            gst[w, p] = rows
            part = nt(rows, pair_cols(vh[own, :], vl[own, :], p), None)
            dattn[w, :, p * 32 : p * 32 + 32, :] = part.reshape(WLON, 32, ROWS)

    nothing = jnp.zeros((BLOCK, 128), F32)
    for w in range(PW):
        turns = [None] * 8
        for x in range(WLON):
            s = scores[w, x] + strip[w, x]
            e = jnp.exp(s - jnp.max(s, axis=1, keepdims=True))
            a = e * (1.0 / jnp.sum(e, axis=1, keepdims=True))
            da = dattn[w, x]
            ds = a * (da - jnp.sum(a * da, axis=1, keepdims=True))
            ah[w, x], al[w, x] = split(a, 2)
            dh[w, x], dl[w, x] = split(ds, 2)
            turn, tile = (WLON - 1 - x) % 8, (WLON - 1 - x) // 8
            two = jnp.concatenate([ds, jnp.zeros((BLOCK, 256 - ROWS), F32)], axis=1)
            wide = jnp.concatenate([nothing, two] if tile else [two, nothing], axis=1)
            turns[turn] = wide if turns[turn] is None else turns[turn] + wide
        dband = turns[0]
        for turn in range(1, 8):
            dband = dband + pltpu.roll(turns[turn], turn * GROUP, 1)
        turned[:, :BLOCK] = dband.T
        for n in range(POS):
            row = (n // WLAT) * 8 + n % WLAT
            lanes[pl.ds(w * 24, 24), n * 128 : n * 128 + 128] = turned[pl.ds(row, 24, stride=GROUP), :]

    perm = perm_ref[...]
    sums = sum(nn(part, perm, None) for part in split(lanes[...], 2))
    for t in range(7):
        for q in range(NY):
            bsend[t * NY + q] = sums[q * 12 : (q + 1) * 12, t * 128 : (t + 1) * 128]
    bsend[pl.ds(28, 4)] = jnp.zeros((4, 12, 128), F32)
    step_b = (lon_peers, lon, lambda o: bsend.at[o], brecv, send_b, recv_b)
    exchange(*step_b)

    def pair_of(ref, w, p):
        return ref[w, :, p * 32 : p * 32 + 32, :].reshape(PSTACK, ROWS)

    def applied(high, low, other_high, other_low):
        result = []
        for w, own in enumerate(windows):
            cols = []
            for p in range(PAIRS_OF_HEADS):
                at = slice(p * LANES, (p + 1) * LANES)
                oh = other_high[own, :][:, at]
                both = nn(pair_of(high, w, p), jnp.concatenate([oh, other_low[own, :][:, at]], axis=1), None)
                rest = nn(pair_of(low, w, p), oh, None)
                cols.append(pick_heads(both[:, :LANES] + both[:, LANES:] + rest))
            result.append(jnp.concatenate(cols, axis=1))
        return jnp.concatenate(result, axis=0)

    def gathered_keys(high, low, stack):
        result = []
        for w in range(PW):
            cols = []
            for p in range(PAIRS_OF_HEADS):
                rows = stack[w, p]
                both = tn(pair_of(high, w, p), rows[:, : 2 * LANES], None)
                rest = tn(pair_of(low, w, p), rows[:, :LANES], None)
                cols.append(both[:, :LANES] + both[:, LANES:] + rest)
            result.append(jnp.concatenate(cols, axis=1))
        return jnp.concatenate(result, axis=0)

    def cut(ref, one, two):
        columns = [
            one[:, :128], two[:, :128],
            jnp.concatenate([one[:, 128:], two[:, 128:]], axis=1),
        ]
        for l in range(LAT):
            for g in range(3):
                ref[l % 2, l // 2, pl.ds(g * 12, 12), :] = columns[g][l * 12 : (l + 1) * 12]

    mixture = applied(ah, al, vh, vl)
    dv = gathered_keys(ah, al, gst)
    hidden = hid[...]
    cut(wsend, tn(hidden, dv), tn(mixture, cot[...]))
    swap = [
        remote(wsend.at[1 - core], wcore, send_c.at[0], recv_c.at[0], partner),
        remote(xsend.at[1 - core], xcore, send_c.at[1], recv_c.at[1], partner),
        remote(nsend, ncore, send_c.at[2], recv_c.at[2], partner),
    ]
    start_all(swap[:1])

    dq = applied(dh, dl, kh, kl) * scale
    step_h = (k_peers, k, lambda o: wsum.at[o], wrecv, send_h, recv_h)
    step_x = (k_peers, k, lambda o: xsum.at[o], xrecv, send_x, recv_x)
    wait_all(swap[:1])
    if comm:
        for o in range(NK):
            wsum[o] = wsend[core, o] + wcore[o]
        exchange(*step_h)
        wrecv[k] = wsum[k]

    dk = gathered_keys(dh, dl, qst)
    cut(xsend, tn(hidden, dq), tn(hidden, dk))
    start_all(swap[1:2])

    gh = nt(dq, wq) + nt(dk, wk) + nt(dv, wv)
    standard = unit[...]
    ggain = jnp.sum(gh * standard, axis=0, keepdims=True)
    gshift = jnp.sum(gh, axis=0, keepdims=True)
    lead = jnp.zeros((4, 32), F32)
    fours = [t[:, u : u + 96] for t in (ggain, gshift) for u in (0, 96)]
    nsend[...] = jnp.concatenate([lead, jnp.concatenate(fours, axis=0)], axis=1)
    start_all(swap[2:])
    wait_all(swap[1:2])
    if comm:
        for o in range(NK):
            xsum[o] = xsend[core, o] + xcore[o]
        exchange(*step_x)
        xrecv[k] = xsum[k]

    mine_z = pl.ds(z * NY, NY)
    y_peers = [(lon_of(0, i), {"lon": lon_of(0, i)}) for i in FAR_FIRST[NY]]
    step_g = (y_peers, lon, lambda o: gathered.at[lon], gathered, send_g, recv_g)
    gu = gh * gain
    mean_gu = jnp.sum(gu, axis=1, keepdims=True) * (1.0 / D)
    mean_uu = jnp.sum(gu * standard, axis=1, keepdims=True) * (1.0 / D)
    grad_ref[...] = cot[...] + inv[...] * (gu - mean_gu - standard * mean_uu)
    for d, base in ((0, 0), (1, 3 * HROWS)):
        cells = [grad_ref[pl.ds(base + g * 8, WLAT), :] for g in range(PIECES)]
        for g in range(PIECES):
            back_out[d, g] = cells[g][:, :128]
        for g in range(HALF):
            back_out[d, PIECES + g] = jnp.concatenate([cells[g][:, 128:], cells[HALF + g][:, 128:]], axis=1)
    backs = [
        remote(back_out.at[d], piece.at[d], send_p.at[4 + d], recv_p.at[4 + d], (left, right)[d])
        for d in range(2)
    ]
    start_all(backs)
    if not comm:
        gathered[...] = bsend[...]
        spare[0] = wsend[...]
        spare[1] = xsend[...]
        last[0:4, :] = nsend[...]
        return

    wait_all(swap[2:])
    step_n = (k_peers, k, lambda o: nsum, nrecv, send_n, recv_n)
    nsum[...] = nsend[...] + ncore[...]
    exchange(*step_n)
    nrecv[k] = nsum[...]

    if comm:
        brecv[lon] = bsend[lon]
        finish(*step_b)
        gathered[lon] = total(brecv, NLON)
        exchange(*step_g)

    step_l = (lon_peers, lon, lambda o: zsend.at[o], zrecv, send_l, recv_l)

    finish(*step_h)
    block_vo = total(wrecv, NK)
    finish(*step_n)
    norm = jnp.concatenate([total(nrecv, NK), jnp.zeros((4, 128), F32)], axis=0)
    lane = lax.broadcasted_iota(jnp.int32, (12, 128), 1)
    lane8 = lax.broadcasted_iota(jnp.int32, (8, 128), 1)
    row8 = lax.broadcasted_iota(jnp.int32, (8, 128), 0)
    block = block_vo
    for t in (4, 5, 6, 7, 0, 1, 2, 3):
        if t == 0:
            finish(*step_x)
            block = total(xrecv, NK)
        e = (t // 2) % 2
        main = block[e * 12 : e * 12 + 12]
        if t % 2:
            tail = pltpu.roll(block[24:36], 96 if e else 32, 1)
            main = jnp.where(lane < 32, pltpu.roll(main, 32, 1), tail)
        top, low = main[0:8], main[4:12]
        for q in range(NY):
            above = top if q == 0 else pltpu.roll(top, 128 - 24 * q, 1)
            below = pltpu.roll(low, (160 - 24 * q) % 128, 1)
            zsend[t * NY + q] = jnp.where(lane8 < 24, above, jnp.where(row8 < 4, norm, below))
    exchange(*step_l)
    zrecv[lon] = zsend[lon]

    finish(*step_g)
    spread_z = [
        (remote(gathered.at[mine_z], gathered.at[mine_z], send_s.at[i], recv_s.at[z], {"lon": lon_of(dz, 0)}), dz)
        for i, dz in enumerate(FAR_FIRST[NZ])
    ]
    for copy, _ in spread_z:
        copy.start()

    wait_all(backs)
    for i, (copy, dz) in list(enumerate(spread_z))[::-1]:
        other = lax.rem(z + dz, NZ)
        theirs = pl.ds(other * NY, NY)
        remote(gathered.at[theirs], gathered.at[theirs], send_s.at[i], recv_s.at[other], {"lon": lon_of(dz, 0)}).wait_recv()
        copy.wait_send()
    finish(*step_l)
    last[...] = total(zrecv, NLON)


def main_call(comm, operands):
    vmem = pl.BlockSpec(memory_space=pltpu.VMEM)
    hbm = pl.BlockSpec(memory_space=pltpu.HBM)
    dma = pltpu.SemaphoreType.DMA
    sems = []
    for n in (6, 3, NK, NK, NK, NLON, NLON, NZ, NLON):
        sems += [dma((n,)), dma((n,))]

    def buf(*shape):
        return pltpu.VMEM(shape, F32)

    def half(*shape):
        return pltpu.VMEM(shape, BF16)

    full = buf(PW * ROWS, D)
    token = half(PW * ROWS, D)
    stack = half(PW, PAIRS_OF_HEADS, PSTACK, 3 * LANES)
    square = (PW, WLON, BLOCK, ROWS)
    outs = (
        jax.ShapeDtypeStruct((PW * ROWS, D), F32),
        jax.ShapeDtypeStruct((PW, PIECES + HALF, WLAT, 128), F32),
        jax.ShapeDtypeStruct((NLON, 12, 128), F32),
        jax.ShapeDtypeStruct((8, 128), F32),
    )
    params = dict(vmem_limit_bytes=VLIM)
    if comm:
        params.update(collective_id=0, has_side_effects=True)
    else:
        outs += (jax.ShapeDtypeStruct((2, 2, NK, 36, 128), F32),)
    return pl.pallas_call(
        functools.partial(main_kernel, comm),
        out_shape=outs,
        in_specs=[hbm] * 8,
        out_specs=(vmem,) * len(outs),
        scratch_shapes=[pltpu.VMEM(t.shape, t.dtype) for t in operands] + [
            dma((8,)),
            buf(2, 3 * PIECES, WLAT, 128), buf(2, 3 * PIECES, WLAT, 128), buf(3, PW * ROWS, 128),
            buf(2, PIECES + HALF, WLAT, 128),
            full, full, buf(PW * ROWS, 1), full,
            token, token, token, token, token, token, token, token,
            buf(*square), buf(STRIP, 128), stack, stack, buf(*square), buf(*square),
            half(*square), half(*square), half(*square), half(*square), buf(48, POS * 128),
            buf(2, NK, 36, 128), buf(2, NK, 36, 128), buf(4, 128), buf(NLON, 12, 128),
            buf(NK, 36, 128), buf(NK, 36, 128), buf(4, 128),
            buf(NK, 36, 128), buf(NK, 36, 128), buf(NK, 36, 128), buf(NK, 36, 128), buf(4, 128), buf(NK, 4, 128),
            buf(NLON, 12, 128), buf(NLON, 8, 128), buf(NLON, 8, 128),
        ] + sems,
        compiler_params=pltpu.CompilerParams(**params),
        name="window_block",
    )(*(pltpu.with_memory_space_constraint(t, pltpu.HBM) for t in operands))


def unpack_kernel(grad_ref, piece, gathered, last, feat_ref, weight_ref, bias_ref, norm_ref):
    for x in range(HALF):
        for c, slabs in ((0, (3, 0)), (1, (1, 2))):
            for i, slab in enumerate(slabs):
                row = x * GROUP + i * 8
                own = grad_ref[pl.ds((1 + c) * HROWS + row, 8), :]
                g = x * 2 + i
                side = piece[c, PIECES + g % HALF]
                side = side[:, :64] if g < HALF else side[:, 64:]
                own, far = own[:WLAT], jnp.concatenate([piece[c, g], side], axis=1)
                west, east = (own, far) if c == 0 else (far, own)
                feat_ref[:, x, slab, :] = west
                feat_ref[:, HALF + x, slab, :] = east
    for h in range(HEADS):
        for q in range(NY):
            rows = 12 if q % 2 == 0 else LONREL - 12
            at = pl.ds(12 * (q % 2), rows)
            rem = gathered[24 + q]
            rem = rem if h == 0 else pltpu.roll(rem, 128 - 16 * h, 1)
            bias_ref[h, at, q // 2, 0:128] = gathered[h * NY + q][:rows]
            bias_ref[h, at, q // 2, 128:144] = rem[:rows, :16]
    both = last[...] * (1.0 / 384.0)
    weight_ref[0:8, :] = both[:, 0:24]
    weight_ref[8:12, :] = both[4:8, 32:56]
    for e in range(2):
        norm_ref[e : e + 1, 0:96] = both[2 * e : 2 * e + 1, 32:128]
        norm_ref[e : e + 1, 96:192] = both[2 * e + 1 : 2 * e + 2, 32:128]


def unpack(operands):
    vmem = pl.BlockSpec(memory_space=pltpu.VMEM)
    return pl.pallas_call(
        unpack_kernel,
        out_shape=(
            jax.ShapeDtypeStruct((WLAT, WLON, 4, D), F32),
            jax.ShapeDtypeStruct((12, 24), F32),
            jax.ShapeDtypeStruct((HEADS, LONREL, PW, PAIRS), F32),
            jax.ShapeDtypeStruct((2, D), F32),
        ),
        in_specs=[vmem] * 4,
        out_specs=(vmem,) * 4,
        compiler_params=pltpu.CompilerParams(vmem_limit_bytes=8 * 1024 * 1024),
        name="unpack",
    )(*operands)


def operands_of(features, cotangent, norm_gain, norm_shift, qkv_weight, out_weight, bias_table):
    return (
        features.transpose(1, 2, 0, 3),
        cotangent.transpose(1, 2, 0, 3),
        norm_gain.reshape(1, D),
        norm_shift.reshape(1, D),
        qkv_weight,
        out_weight,
        bias_table.reshape(PW, HEADS, LONREL, PAIRS).transpose(1, 2, 0, 3),
        jnp.asarray(permutation(), jnp.bfloat16),
    )


def shards(*args):
    grad_features, grad_weights, grad_bias, grad_norm = unpack(main_call(True, operands_of(*args)))
    return (
        grad_features.transpose(2, 0, 1, 3),
        grad_weights,
        grad_bias.transpose(2, 0, 1, 3).reshape(1, PW, HEADS, LONREL, PAIRS),
        grad_norm,
    )


def solution(mesh):
    placed = (
        P(None, "lat", "lon", None),
        P(None, "lat", "lon", None),
        P(),
        P(),
        P(),
        P(),
        P("lat", None, None, None, None),
    )
    return jax.shard_map(
        shards,
        mesh=mesh,
        in_specs=placed,
        out_specs=(
            P(None, "lat", "lon", None),
            P("lat", "lon"),
            P("lat", None, None, None, None),
            P(),
        ),
        check_vma=False,
    )
```
